32 devices in a mesh: tgt: 4 (over z), ptr: 8 (over y, x, core).
Axes of the slice: x: 2, y: 2, z: 4, core: 2. Of those that a mesh axis runs over, the one named last changes fastest.
Arguments:
- targets: float32 [32, 32, 1024], P('tgt'), may hold values from -12 to 12
- partners: float32 [32, 32, 1024], P(None, None, 'ptr'), may hold values from -6 to 6
- occupied: int32 [8], P('ptr'), may hold values 0 or 1
- retained: int32 [1], replicated, may hold values from 16 to 32
Outputs:
- compressed: float32 [32, 32, 1024], P('tgt', 'ptr')
The draws below stay inside these ranges and needn't reach their ends.
All inputs are finite; a program needn't handle non-finite values. No bound on the sum of `occupied` on one device may be relied on, other than what follows from the above.
Results may differ from the reference program's by a relative error of at most 0.00008.
Values sent between devices are 32-bit elements; how exact they have to be, the bound alone decides.
A program may use at most 64 MiB of HBM per device.

```python
import math
import jax
import jax.numpy as jnp
from jax import lax

NG = 32
NT = 32
NP = 32
NBLK = 8


def draw_targets(key, part):
    key_base = jax.random.fold_in(key, 11)
    key_mixing = jax.random.fold_in(key, 12)
    key_planes = jax.random.fold_in(key, 13)
    fields = jax.random.normal(key_base, (NT, NG, NG * NG), jnp.float32)
    mixing = 0.09 * jax.random.normal(key_mixing, (NT, NT), jnp.float32)
    mixing = mixing + jnp.eye(NT, dtype=jnp.float32)
    rising = jnp.arange(NG).astype(jnp.float32) / (NG - 1)
    envelope = jnp.exp(rising * 1.0986123) * jax.random.uniform(key_planes, (NG,), jnp.float32, 0.7, 1.4)
    mixed = jnp.einsum('ab,bxm->axm', mixing, fields, precision=jax.lax.Precision.HIGHEST)
    return jnp.clip(mixed * envelope[None, :, None], -12.0, 12.0)


def place_ends(array, stream_key, low, top_value):
    longest = array.shape.index(max(array.shape))
    spots = []
    for shift in (0, 1):
        where = [jax.random.randint(jax.random.fold_in(stream_key, axis), (), 0, length) for axis, length in enumerate(array.shape)]
        where[longest] = (where[longest] + shift) % array.shape[longest]
        spots.append(tuple(where))
    return array.at[spots[0]].set(low).at[spots[1]].set(top_value)


def shard_levels(own_key, extent, split, low, largest):
    loudness = 1.0
    for position, shards_of in split:
        draws = jax.random.uniform(jax.random.fold_in(jax.random.fold_in(own_key, 6), position), (shards_of,), jnp.float32, low / len(split), largest / len(split))
        loudness = loudness * jnp.repeat(jnp.exp(draws), extent[position] // shards_of).reshape((-1,) + (1,) * (len(extent) - 1 - position))
    return loudness


def scatter_about(stream_key, extent, width, reach, cuts=(), held_as=jnp.bfloat16):
    factor_of = shard_levels(stream_key, extent, cuts, -0.22, 0.18) if cuts else 1.0
    drawn = jax.random.normal(stream_key, extent, jnp.float32) * width * factor_of
    return jnp.minimum(jnp.maximum(drawn, -reach), reach).astype(held_as)


def setup_inputs(seed: int = 0) -> dict:
    seeds = jax.random.split(jax.random.key(seed), 5)
    return {
        "targets": draw_targets(jax.random.fold_in(seeds[4], 71), 0),
        "partners": scatter_about(seeds[1], (NG, NG, NP * NG), 1.0, 6.0, ((2, 8),), jnp.float32),
        "occupied": place_ends((jax.random.randint(seeds[2], (NBLK,), 0, 4) < 3).astype(jnp.int32), jax.random.fold_in(seeds[2], 1), 0, 1),
        "retained": jax.random.randint(seeds[3], (1,), NT // 2, NT + 1).astype(jnp.int32),
    }


def coulomb_table(length):
    indices = jnp.arange(length, dtype=jnp.int32)
    signed = jnp.where(indices < length // 2, indices, indices - length).astype(jnp.float32)
    wave = signed * (2.0 * math.pi / length)
    wave = wave * wave
    total = wave[:, None, None] + wave[None, :, None] + wave[None, None, :]
    safe = jnp.where(total > 0.0, total, jnp.float32(1.0))
    return jnp.where(total > 0.0, 4.0 * math.pi / safe, jnp.float32(0.0))

def reference(targets, partners, occupied, retained):
    ncells = NG * NG * NG
    coulomb = coulomb_table(NG)
    orbitals = jnp.transpose(partners.reshape(NG, NG, NP, NG), (2, 0, 1, 3))
    occupancy = 0.25 + 0.75 * jnp.repeat(occupied.astype(jnp.float32), 4)
    weighted = orbitals * occupancy[:, None, None, None]

    def action(target_one):
        density = target_one.reshape(NG, NG, NG)[None] * orbitals
        spectrum = jnp.fft.fftn(density, axes=(1, 2, 3))
        potential = jnp.real(jnp.fft.ifftn(spectrum * coulomb[None], axes=(1, 2, 3)))
        return jnp.sum(weighted * potential, axis=0).reshape(NG, NG * NG)
    actions = lax.map(action, targets)
    intersection = jnp.einsum('axm,bxm->ab', targets, actions, precision=lax.Precision.HIGHEST) / ncells
    lower = jnp.linalg.cholesky(intersection)
    inverse = jax.scipy.linalg.solve_triangular(lower, jnp.eye(NT, dtype=jnp.float32), lower=True)
    result = jnp.einsum('bc,cxm->bxm', inverse, actions, precision=lax.Precision.HIGHEST)
    keeping = (jnp.arange(NT, dtype=jnp.int32) < retained[0]).astype(jnp.float32)
    return result * keeping[:, None, None]
```

```python
import functools
import math

import jax
import jax.numpy as jnp
import numpy as np
from jax import lax
from jax.experimental import pallas as pl
from jax.experimental.pallas import tpu as pltpu
from jax.sharding import PartitionSpec as P

HIGHEST = lax.Precision.HIGHEST
MESH = pl.DeviceIdType.MESH
FORWARD = 4
BACKWARD = 4
PIVOTS = 4


def real_dft(values):
    n = len(values)
    if n == 1:
        return [values[0]], [None]
    even_re, even_im = real_dft(values[0::2])
    odd_re, odd_im = real_dft(values[1::2])
    half = n // 2
    re, im = [None] * (half + 1), [None] * (half + 1)
    re[0], re[half] = even_re[0] + odd_re[0], even_re[0] - odd_re[0]
    for k in range(1, half // 2 + 1):
        if 2 * k == half:
            re[k], im[k] = even_re[k], -odd_re[k]
            continue
        c, s = math.cos(2 * math.pi * k / n), -math.sin(2 * math.pi * k / n)
        if 8 * k == n:
            a = c * (odd_re[k] + odd_im[k]) if odd_im[k] is not None else c * odd_re[k]
            b = c * (odd_im[k] - odd_re[k]) if odd_im[k] is not None else -c * odd_re[k]
        else:
            a = c * odd_re[k] - s * odd_im[k]
            b = s * odd_re[k] + c * odd_im[k]
        re[k], re[half - k] = even_re[k] + a, even_re[k] - a
        im[k], im[half - k] = even_im[k] + b, b - even_im[k]
    return re, im


def real_dft_transposed(re, im):
    half = len(re) - 1
    if half == 0:
        return [re[0]]
    n = 2 * half
    quarter = half // 2
    even_re, even_im = [None] * (quarter + 1), [None] * (quarter + 1)
    odd_re, odd_im = [None] * (quarter + 1), [None] * (quarter + 1)
    even_re[0], odd_re[0] = re[0] + re[half], re[0] - re[half]
    for k in range(1, quarter + 1):
        if 2 * k == half:
            even_re[k], odd_re[k] = re[k], -im[k]
            continue
        c, s = math.cos(2 * math.pi * k / n), -math.sin(2 * math.pi * k / n)
        even_re[k], even_im[k] = re[k] + re[half - k], im[k] - im[half - k]
        a, b = re[k] - re[half - k], im[k] + im[half - k]
        if 8 * k == n:
            odd_re[k], odd_im[k] = c * (a - b), c * (a + b)
        else:
            odd_re[k], odd_im[k] = c * a + s * b, c * b - s * a
    values = [None] * n
    values[0::2] = real_dft_transposed(even_re[: quarter + 1], even_im[: quarter + 1])
    values[1::2] = real_dft_transposed(odd_re[: quarter + 1], odd_im[: quarter + 1])
    return values


def flat_dft(values):
    re, im = real_dft(values)
    return re + im[1:-1]


def flat_dft_transposed(modes):
    half = len(modes) // 2
    return real_dft_transposed(modes[: half + 1], [None] + modes[half + 1 :] + [None])


def split_product(field, weights):
    width = field.shape[1]
    high = field.astype(jnp.bfloat16)
    low = (field - high.astype(jnp.float32)).astype(jnp.bfloat16)
    both = jnp.dot(
        jnp.concatenate([high, low], axis=1), weights, preferred_element_type=jnp.float32
    )
    return both[:, :width] + both[:, width:]


def kernel(
    tn, pn, t_hbm, psi_hbm, weights_hbm, table_hbm, occupied_ref, retained_ref, out_ref,
    planes, psi_ref, weights_ref, table_ref, spec, part, pair_buf, rs_buf, t_buf, a_buf,
    gram_ref, g_buf, inv_ref,
):
    slab = planes.shape[0] // pn
    rows = planes.shape[1]
    dma = pltpu.SemaphoreType.DMA
    pl.run_scoped(
        functools.partial(
            exchange, tn, pn, t_hbm, psi_hbm, weights_hbm, table_hbm, occupied_ref, retained_ref,
            out_ref, planes, psi_ref, weights_ref, table_ref, spec, part, pair_buf, rs_buf, t_buf,
            a_buf, gram_ref, g_buf, inv_ref,
        ),
        dma((2, rows)), dma((4,)), dma((pn // 2, slab)), dma((pn // 2, slab)),
        dma((pn // 2, slab)), dma((pn // 2, slab)), dma((tn,)), dma((tn,)),
        dma((tn, tn, slab)), dma((tn, slab)), dma((tn,)), dma((tn,)),
    )


def exchange(
    tn, pn, t_hbm, psi_hbm, weights_hbm, table_hbm, occupied_ref, retained_ref, out_ref,
    planes, psi_ref, weights_ref, table_ref, spec, part, pair_buf, rs_buf, t_buf, a_buf,
    gram_ref, g_buf, inv_ref,
    plane_sem, load_sem, pair_send, pair_recv, rs_send, rs_recv, t_send, t_recv,
    a_send, a_recv, g_send, g_recv,
):
    t, p = lax.axis_index("tgt"), lax.axis_index("ptr")
    length, rows, cells = planes.shape
    lanes = psi_ref.shape[2]
    groups = lanes // length
    slab = length // pn
    all_cells = length * cells
    total_rows = tn * rows
    width = inv_ref.shape[1]
    me = t * pn + p
    chips = pn // 2
    chip, core = p // 2, lax.rem(p, 2)
    partner = p + 1 - 2 * core
    early = length // 4

    def plane_load(c, a):
        xs = pl.ds(0, early) if c == 0 else pl.ds(early, length - early)
        return pltpu.make_async_copy(t_hbm.at[a, xs, :], planes.at[xs, a, :], plane_sem.at[c, a])

    def psi_load(c):
        xs = pl.ds(0, early) if c == 0 else pl.ds(early, length - early)
        return pltpu.make_async_copy(psi_hbm.at[xs], psi_ref.at[xs], load_sem.at[c])

    weights_load = pltpu.make_async_copy(weights_hbm, weights_ref, load_sem.at[2])
    table_load = pltpu.make_async_copy(table_hbm, table_ref, load_sem.at[3])

    weights_load.start()
    for c in range(2):
        psi_load(c).start()
        for a in range(rows):
            plane_load(c, a).start()
    table_load.start()

    barrier = pltpu.get_barrier_semaphore()
    for tt in range(tn):
        for pp in range(pn):

            @pl.when((t != tt) | (p != pp))
            def greet():
                pl.semaphore_signal(barrier, inc=1, device_id=(tt, pp), device_id_type=MESH)

    def pair_copy(q, r):
        return pltpu.make_async_remote_copy(
            src_ref=part.at[q * slab + r], dst_ref=pair_buf.at[q // 2, r],
            send_sem=pair_send.at[q // 2, r], recv_sem=pair_recv.at[q // 2, r],
            device_id=(t, partner), device_id_type=MESH,
        )

    def rs_copy(c, slot, r):
        q = 2 * c + core
        return pltpu.make_async_remote_copy(
            src_ref=part.at[q * slab + r], dst_ref=rs_buf.at[slot, r],
            send_sem=rs_send.at[c, r], recv_sem=rs_recv.at[slot, r],
            device_id=(t, q), device_id_type=MESH,
        )

    def t_copy(d, source, target):
        return pltpu.make_async_remote_copy(
            src_ref=planes.at[pl.ds(p * slab, slab)], dst_ref=t_buf.at[source],
            send_sem=t_send.at[d], recv_sem=t_recv.at[d],
            device_id=(target, p), device_id_type=MESH,
        )

    def t_sends(act):
        for d in range(1, tn):
            target = t + d if d % 2 else t - d

            @pl.when((target >= 0) & (target < tn))
            def send():
                act(t_copy(d, t, target))

    def t_arrivals():
        for d in range(1, tn):
            source = t - d if d % 2 else t + d

            @pl.when((source >= 0) & (source < tn))
            def arrived():
                t_copy(d, source, t).wait_recv()

    def a_copy(s, target, r):
        return pltpu.make_async_remote_copy(
            src_ref=a_buf.at[s, r], dst_ref=a_buf.at[s, r],
            send_sem=a_send.at[s, target, r], recv_sem=a_recv.at[s, r],
            device_id=(target, p), device_id_type=MESH,
        )

    def a_route(r, act):
        for s in range(tn - 1):
            for target in range(s + 1, tn):
                if s % 2 == 0 or target == s + 1:

                    @pl.when(t == s)
                    def direct():
                        act(a_copy(s, target, r))

    def a_onward(r, act, wait):
        for s in range(1, tn - 2, 2):

            @pl.when(t == s + 1)
            def onward():
                if wait:
                    a_copy(s, s + 1, r).wait_recv()
                for target in range(s + 2, tn):
                    act(a_copy(s, target, r))

    def a_arrivals():
        for s in range(tn - 1):
            if s % 2 == 1 and s + 2 < tn:
                here = t > s + 1
            else:
                here = t > s

            @pl.when(here)
            def arrived():
                for r in range(slab):
                    a_copy(s, s + 1, r).wait_recv()

    def start(copy):
        copy.start()

    def sent(copy):
        copy.wait_send()

    def g_copy(target, q):
        return pltpu.make_async_remote_copy(
            src_ref=g_buf.at[me], dst_ref=g_buf.at[me],
            send_sem=g_send.at[target], recv_sem=g_recv.at[t],
            device_id=(target, q), device_id_type=MESH,
        )

    def g_all(s, count):
        every = g_buf.at[pl.ds(s * pn, count)]
        return pltpu.make_async_remote_copy(
            src_ref=every, dst_ref=every, send_sem=g_send.at[s], recv_sem=g_recv.at[s],
            device_id=(t, partner), device_id_type=MESH,
        )

    group_of = lax.broadcasted_iota(jnp.int32, (rows, lanes), 1) // length
    at_group = [group_of == g for g in range(groups)]
    per_block = groups // occupied_ref.shape[0]
    occ = 0.25 + 0.75 * occupied_ref[0].astype(jnp.float32) * jnp.ones((rows, lanes), jnp.float32)
    for i in range(1, occupied_ref.shape[0]):
        level = 0.25 + 0.75 * occupied_ref[i].astype(jnp.float32)
        occ = jnp.where(group_of >= i * per_block, level, occ)

    def pick(options):
        chosen = options[0]
        for g in range(1, groups):
            chosen = jnp.where(at_group[g], options[g], chosen)
        return chosen

    def rolled(value, steps):
        steps = steps % groups
        return value if steps == 0 else pltpu.roll(value, steps * length, 1)

    plane_rows = length * rows

    weights_load.wait()
    psi_load(0).wait()
    for a in range(rows):
        plane_load(0, a).wait()

    @pl.loop(0, length // FORWARD)
    def forward(i):
        @pl.when(i == early // FORWARD)
        def rest():
            psi_load(1).wait()
            for a in range(rows):
                plane_load(1, a).wait()

        density = []
        for j in range(FORWARD):
            x = i * FORWARD + j
            for q in range(length // groups):
                v = planes[x, :, q * lanes : (q + 1) * lanes]
                turned = [rolled(v, s) for s in range(groups)]
                for g in range(groups):
                    y = q * groups + g
                    spread = pick([turned[(h - g) % groups] for h in range(groups)])
                    density.append(spread * psi_ref[x, y : y + 1, :])
        waves = split_product(jnp.concatenate(density, axis=0), weights_ref[...])
        for j in range(FORWARD):
            wave = waves[j * plane_rows : (j + 1) * plane_rows]
            modes = flat_dft([wave[y * rows : (y + 1) * rows] for y in range(length)])
            for m in range(length):
                spec[i * FORWARD + j, m] = modes[m]

    t_buf[t] = planes[pl.ds(p * slab, slab)]
    for s in range(1, tn):

        @pl.when(s > t)
        def clear():
            a_buf[s] = jnp.zeros(a_buf.shape[1:], jnp.float32)

    gram_ref[...] = jnp.zeros_like(gram_ref)
    table_load.wait()
    pl.semaphore_wait(barrier, tn * pn - 1)
    t_sends(start)

    @pl.loop(0, length)
    def middle(m):
        modes = flat_dft([spec[x, m] for x in range(length)])
        half = length // 2
        scaled = []
        for i in range(length):
            k = i if i <= half else i - half
            scaled.append(modes[i] * table_ref[m, k : k + 1, :])
        values = flat_dft_transposed(scaled)
        for x in range(length):
            spec[x, m] = values[x]

    per = chips // BACKWARD

    @pl.loop(0, 2 * slab * per)
    def backward(n):
        i = n // per
        first = lax.rem(n, per) * BACKWARD
        odd = lax.rem(i, 2)
        last = i == 2 * slab - 1
        away = (i == 0) | ((odd == 1) & jnp.logical_not(last))
        r = jnp.where(away, (i + 1) // 2, jnp.where(last, slab - 1, i // 2 - 1))
        side = jnp.where(away, 1 - core, core)
        owners = [2 * lax.rem(chip + 1 + first + j, chips) + side for j in range(BACKWARD)]
        values = []
        for q in owners:
            values += flat_dft_transposed([spec[q * slab + r, m] for m in range(length)])
        potentials = split_product(jnp.concatenate(values, axis=0), weights_ref[...])
        for j, owner in enumerate(owners):
            x = owner * slab + r
            potential = potentials[j * plane_rows : (j + 1) * plane_rows]
            for q in range(length // groups):
                terms = []
                for g in range(groups):
                    y = q * groups + g
                    terms.append(potential[y * rows : (y + 1) * rows] * psi_ref[x, y : y + 1, :])
                total = None
                for s in range(groups):
                    chosen = pick([terms[(h - s) % groups] for h in range(groups)])
                    moved = rolled(chosen * occ, -s)
                    total = moved if total is None else total + moved
                part[x, :, q * lanes : (q + 1) * lanes] = total

        @pl.when(away)
        def to_partner():
            for owner in owners:
                pair_copy(owner, r).start()

        @pl.when(jnp.logical_not(away))
        def to_owners():
            for j, owner in enumerate(owners):
                pair_copy(owner, r).wait_recv()

                @pl.when(first + j < chips - 1)
                def send():
                    x = owner * slab + r
                    part[x] = part[x] + pair_buf[owner // 2, r]
                    rs_copy(owner // 2, chip, r).start()

    t_arrivals()

    @pl.loop(0, slab)
    def reduce(r):
        own = part[p * slab + r] + pair_buf[chip, r]
        for d in range(1, chips):
            c = lax.rem(chip + d, chips)
            rs_copy(c, c, r).wait_recv()
            own = own + rs_buf[c, r]
        a_buf[t, r] = own
        a_route(r, start)
        every = jnp.concatenate([t_buf[s, r] for s in range(tn)], axis=0)
        gram_ref[...] += lax.dot_general(
            own, every, (((1,), (1,)), ((), ())),
            precision=HIGHEST, preferred_element_type=jnp.float32,
        )

        @pl.when(r > 0)
        def earlier():
            a_onward(r - 1, start, True)

    gram = gram_ref[...] * (1.0 / all_cells)
    fold = 128 // total_rows
    short = rows // fold
    g_buf[me] = jnp.concatenate([gram[i * short : (i + 1) * short] for i in range(fold)], axis=1)

    for target in reversed(range(tn)):
        for q in range(pn):

            @pl.when((t < target) | ((t == target) & (p != q)))
            def spread():
                g_copy(target, q).start()

    a_onward(slab - 1, start, True)
    t_sends(sent)

    @pl.loop(0, slab)
    def drain(r):
        for c in range(chips):
            pair_copy(2 * c + 1 - core, r).wait_send()
        for d in range(1, chips):
            rs_copy(lax.rem(chip + d, chips), chip, r).wait_send()

    for s in range(tn):

        @pl.when(t > s)
        def others():
            g_all(s, pn).wait_recv()

        @pl.when(t == s)
        def mates():
            g_all(s, pn - 1).wait_recv()

    blocks = []
    for s in range(tn):
        block = g_buf[s * pn]
        for q in range(1, pn):
            block = block + g_buf[s * pn + q]
        blocks += [block[:, i * total_rows : (i + 1) * total_rows] for i in range(fold)]
    square = jnp.concatenate(blocks, axis=0)
    square = jnp.concatenate(
        [square, jnp.zeros((total_rows, width - total_rows), jnp.float32)], axis=1
    )
    row_of = lax.broadcasted_iota(jnp.int32, (total_rows, width), 0)
    lane_of = lax.broadcasted_iota(jnp.int32, (total_rows, width), 1)
    row_block, lane_block = row_of // rows, lane_of // rows
    apart = lane_block - row_block
    odd = lax.rem(jnp.abs(apart), 2) == 1
    held = (apart == 0) | ((apart < 0) & odd) | ((apart > 0) & jnp.logical_not(odd))
    held = held & (row_block <= t) & (lane_block <= t)
    square = jnp.where(held, square, 0.0)
    padded = jnp.concatenate([square, jnp.zeros((width - total_rows, width), jnp.float32)], axis=0)
    both = square + jnp.transpose(padded)[:total_rows]
    symmetric = jnp.where(apart == 0, 0.5 * both, both)
    unit = (lane_of == row_of + total_rows) | ((lane_of == row_of) & (row_block > t))
    work = jnp.where(unit, 1.0, symmetric)
    scale = jnp.zeros((total_rows, width), jnp.float32)
    for k in range(0, total_rows, PIVOTS):
        columns = [
            jnp.broadcast_to(work[:, k + i : k + i + 1], (total_rows, width)) for i in range(PIVOTS)
        ]
        lines = [work[k + i : k + i + 1, :] for i in range(PIVOTS)]
        corner = [[columns[j][k + i : k + i + 1, :] for j in range(PIVOTS)] for i in range(PIVOTS)]
        for i in range(PIVOTS):
            pivot = corner[i][i]
            scale = jnp.where(row_of == k + i, 1.0 / jnp.sqrt(pivot), scale)
            inverse = 1.0 / pivot
            scaled = lines[i] * inverse
            for m in range(i + 1, PIVOTS):
                factor = corner[i][m] * inverse
                columns[m] = columns[m] - columns[i] * factor
                lines[m] = lines[m] - corner[m][i] * scaled
                for h in range(i + 1, PIVOTS):
                    corner[h][m] = corner[h][m] - corner[h][i] * factor
            work = work - jnp.where(row_of > k + i, columns[i], 0.0) * scaled
    keeping = (row_of < retained_ref[0]).astype(jnp.float32)
    inv_ref[...] = work * scale * keeping
    mine = inv_ref[pl.ds(pl.multiple_of(t * rows, rows), rows), :][:, total_rows : 2 * total_rows]
    a_arrivals()
    for x in range(slab):
        every = jnp.concatenate([a_buf[s, x] for s in range(tn)], axis=0)
        out_ref[:, x, :] = jnp.dot(
            mine, every, precision=HIGHEST, preferred_element_type=jnp.float32
        )

    for target in range(tn):

        @pl.when(t < target)
        def upward():
            g_all(target, pn).wait_send()

        @pl.when(t == target)
        def within():
            g_all(target, pn - 1).wait_send()

    for r in range(slab):
        a_route(r, sent)
        a_onward(r, sent, False)


def constants(length, groups):
    i = np.arange(length)
    phase = 2.0 * np.pi / length * (i[:, None] * i[None, :] % length)
    cas = np.kron(np.eye(groups), np.cos(phase) + np.sin(phase)).astype(np.float32)
    high = cas.astype(jnp.bfloat16)
    low = (cas - high.astype(np.float32)).astype(jnp.bfloat16)
    weights = np.concatenate([np.concatenate([high, low], 1)] * 2, 0)
    signed = np.where(i < length // 2, i, i - length)
    half = length // 2
    k = np.arange(half + 1)
    wave = (2.0 * np.pi / length) ** 2
    total = wave * ((k**2)[:, None, None] + (k**2)[None, :, None] + (signed**2)[None, None, :])
    coulomb = np.where(total > 0, 4 * np.pi / np.where(total > 0, total, 1.0), 0.0)
    fold = np.where((k == 0) | (k == half), 1.0, 2.0)
    coulomb = coulomb * fold[:, None, None] * fold[None, :, None] / length**3
    order = np.concatenate([np.arange(half + 1), np.arange(1, half)])
    table = np.tile(coulomb[order], (1, 1, groups)).astype(np.float32)
    return weights, table


def shards(tn, pn, targets, partners, occupied, retained):
    rows, length, cells = targets.shape
    lanes = partners.shape[2]
    groups = lanes // length
    slab = length // pn
    weights, table = constants(length, groups)
    total_rows = tn * rows
    width = -(-2 * total_rows // 128) * 128
    vmem = pl.BlockSpec(memory_space=pltpu.VMEM)
    smem = pl.BlockSpec(memory_space=pltpu.SMEM)
    hbm = pl.BlockSpec(memory_space=pl.ANY)
    planes = pltpu.VMEM((length, rows, cells), jnp.float32)
    block = pltpu.VMEM((tn, slab, rows, cells), jnp.float32)
    received = pltpu.VMEM((pn // 2, slab, rows, cells), jnp.float32)
    return pl.pallas_call(
        functools.partial(kernel, tn, pn),
        out_shape=pltpu.VMEM((rows, slab, cells), jnp.float32),
        in_specs=[hbm, hbm, hbm, hbm, smem, smem],
        out_specs=vmem,
        scratch_shapes=[
            planes,
            pltpu.VMEM(partners.shape, jnp.float32),
            pltpu.VMEM(weights.shape, weights.dtype),
            pltpu.VMEM(table.shape, jnp.float32),
            pltpu.VMEM((length, length, rows, lanes), jnp.float32),
            planes,
            received,
            received,
            block,
            block,
            pltpu.VMEM((rows, total_rows), jnp.float32),
            pltpu.VMEM((tn * pn, rows * total_rows // 128, 128), jnp.float32),
            pltpu.VMEM((total_rows, width), jnp.float32),
        ],
        compiler_params=pltpu.CompilerParams(collective_id=0, has_side_effects=True),
        name="exchange",
    )(targets, partners, jnp.asarray(weights), jnp.asarray(table), occupied, retained)


def solution(mesh):
    return jax.shard_map(
        functools.partial(shards, mesh.shape["tgt"], mesh.shape["ptr"]),
        mesh=mesh,
        in_specs=(P("tgt", None, None), P(None, None, "ptr"), P("ptr"), P()),
        out_specs=P("tgt", "ptr", None),
        check_vma=False,
    )
```

```python
import functools
import math

import jax
import jax.numpy as jnp
import numpy as np
from jax import lax
from jax.experimental import pallas as pl
from jax.experimental.pallas import tpu as pltpu
from jax.sharding import PartitionSpec as P

HIGHEST = lax.Precision.HIGHEST
MESH = pl.DeviceIdType.MESH
FORWARD = 8
BACKWARD = 4
PIVOTS = 4
HELD = 2


def turned_by(n, k, re, im):
    c, s = math.cos(2 * math.pi * k / n), math.sin(2 * math.pi * k / n)
    return c * re + s * im, c * im - s * re


def real_dft(values):
    n = len(values)
    if n == 1:
        return [values[0]], [None]
    if n == 2:
        return [values[0] + values[1], values[0] - values[1]], [None, None]
    half, quarter, eighth = n // 2, n // 4, n // 8
    even_re, even_im = real_dft(values[0::2])
    one_re, one_im = real_dft(values[1::4])
    three_re, three_im = real_dft(values[3::4])
    re, im = [None] * (half + 1), [None] * (half + 1)
    total = one_re[0] + three_re[0]
    re[0], re[half] = even_re[0] + total, even_re[0] - total
    re[quarter], im[quarter] = even_re[quarter], three_re[0] - one_re[0]
    for k in range(1, eighth + 1):
        if 2 * k == quarter:
            c = math.sqrt(0.5)
            a, b = c * (one_re[k] - three_re[k]), c * (one_re[k] + three_re[k])
            re[k], re[half - k] = even_re[k] + a, even_re[k] - a
            im[k], im[half - k] = even_im[k] - b, -b - even_im[k]
            continue
        one = turned_by(n, k, one_re[k], one_im[k])
        three = turned_by(n, 3 * k, three_re[k], three_im[k])
        sum_re, sum_im = one[0] + three[0], one[1] + three[1]
        gap_re, gap_im = one[0] - three[0], one[1] - three[1]
        re[k], re[half - k] = even_re[k] + sum_re, even_re[k] - sum_re
        im[k], im[half - k] = even_im[k] + sum_im, sum_im - even_im[k]
        mirror = quarter - k
        re[quarter + k], re[mirror] = even_re[mirror] + gap_im, even_re[mirror] - gap_im
        im[quarter + k], im[mirror] = -gap_re - even_im[mirror], even_im[mirror] - gap_re
    return re, im


def real_dft_transposed(re, im):
    half = len(re) - 1
    if half == 0:
        return [re[0]]
    if half == 1:
        return [re[0] + re[1], re[0] - re[1]]
    n = 2 * half
    quarter, eighth = half // 2, half // 4
    even_re, even_im = [None] * (quarter + 1), [None] * (quarter + 1)
    one_re, one_im = [None] * (eighth + 1), [None] * (eighth + 1)
    three_re, three_im = [None] * (eighth + 1), [None] * (eighth + 1)
    even_re[0], total = re[0] + re[half], re[0] - re[half]
    even_re[quarter] = re[quarter]
    one_re[0], three_re[0] = total - im[quarter], total + im[quarter]
    for k in range(1, eighth + 1):
        sum_re, even_re[k] = re[k] - re[half - k], re[k] + re[half - k]
        sum_im, even_im[k] = im[k] + im[half - k], im[k] - im[half - k]
        if 2 * k == quarter:
            c = math.sqrt(0.5)
            one_re[k], three_re[k] = c * (sum_re - sum_im), -c * (sum_re + sum_im)
            continue
        mirror = quarter - k
        even_re[mirror], gap_im = re[quarter + k] + re[mirror], re[quarter + k] - re[mirror]
        even_im[mirror] = im[mirror] - im[quarter + k]
        gap_re = -(im[quarter + k] + im[mirror])
        one = sum_re + gap_re, sum_im + gap_im
        three = sum_re - gap_re, sum_im - gap_im
        one_re[k], one_im[k] = turned_by(n, -k, *one)
        three_re[k], three_im[k] = turned_by(n, -3 * k, *three)
    values = [None] * n
    values[0::2] = real_dft_transposed(even_re, even_im)
    values[1::4] = real_dft_transposed(one_re, one_im)
    values[3::4] = real_dft_transposed(three_re, three_im)
    return values


def flat_dft(values):
    re, im = real_dft(values)
    return re + im[1:-1]


def flat_dft_transposed(modes):
    half = len(modes) // 2
    return real_dft_transposed(modes[: half + 1], [None] + modes[half + 1 :] + [None])


def split_product(field, weights):
    width = field.shape[1]
    high = field.astype(jnp.bfloat16)
    low = (field - high.astype(jnp.float32)).astype(jnp.bfloat16)
    both = jnp.dot(
        jnp.concatenate([high, low], axis=1), weights, preferred_element_type=jnp.float32
    )
    return both[:, :width] + both[:, width:]


def kernel(
    tn, pn, t_hbm, psi_hbm, weights_hbm, table_hbm, occupied_ref, retained_ref, out_ref,
    planes, psi_ref, weights_ref, table_ref, spec, part, pair_buf, rs_buf, t_buf, a_buf,
    gram_ref, g_col, g_buf, inv_ref,
):
    slab = planes.shape[0] // pn
    rows = planes.shape[1]
    dma = pltpu.SemaphoreType.DMA
    pl.run_scoped(
        functools.partial(
            exchange, tn, pn, t_hbm, psi_hbm, weights_hbm, table_hbm, occupied_ref, retained_ref,
            out_ref, planes, psi_ref, weights_ref, table_ref, spec, part, pair_buf, rs_buf, t_buf,
            a_buf, gram_ref, g_col, g_buf, inv_ref,
        ),
        dma((2, rows)), dma((4,)), dma((pn // 2, slab)), dma((pn // 2, slab)),
        dma((pn // 2, slab)), dma((pn // 2, slab)), dma((tn,)), dma((tn,)),
        dma((tn, tn, slab)), dma((tn, slab)), dma((tn,)), dma((tn,)), dma, dma,
    )


def exchange(
    tn, pn, t_hbm, psi_hbm, weights_hbm, table_hbm, occupied_ref, retained_ref, out_ref,
    planes, psi_ref, weights_ref, table_ref, spec, part, pair_buf, rs_buf, t_buf, a_buf,
    gram_ref, g_col, g_buf, inv_ref,
    plane_sem, load_sem, pair_send, pair_recv, rs_send, rs_recv, t_send, t_recv,
    a_send, a_recv, g_send, g_recv, share_send, share_recv,
):
    t, p = lax.axis_index("tgt"), lax.axis_index("ptr")
    length, rows, cells = planes.shape
    lanes = psi_ref.shape[2]
    groups = lanes // length
    slab = length // pn
    all_cells = length * cells
    total_rows = tn * rows
    width = inv_ref.shape[1]
    chips = pn // 2
    chip, core = p // 2, lax.rem(p, 2)
    partner = p + 1 - 2 * core
    early = length // 4

    def plane_load(c, a):
        xs = pl.ds(0, early) if c == 0 else pl.ds(early, length - early)
        return pltpu.make_async_copy(t_hbm.at[a, xs, :], planes.at[xs, a, :], plane_sem.at[c, a])

    def psi_load(c):
        xs = pl.ds(0, early) if c == 0 else pl.ds(early, length - early)
        return pltpu.make_async_copy(psi_hbm.at[xs], psi_ref.at[xs], load_sem.at[c])

    weights_load = pltpu.make_async_copy(weights_hbm, weights_ref, load_sem.at[2])
    table_load = pltpu.make_async_copy(table_hbm, table_ref, load_sem.at[3])

    weights_load.start()
    for c in range(2):
        psi_load(c).start()
        for a in range(rows):
            plane_load(c, a).start()
    table_load.start()

    barrier = pltpu.get_barrier_semaphore()
    for tt in range(tn):

        @pl.when(t != tt)
        def column():
            pl.semaphore_signal(barrier, inc=1, device_id=(tt, p), device_id_type=MESH)

    for d in range(1, pn):
        pl.semaphore_signal(
            barrier, inc=1, device_id=(t, lax.rem(p + d, pn)), device_id_type=MESH
        )

    def pair_copy(q, r):
        return pltpu.make_async_remote_copy(
            src_ref=part.at[q * slab + r], dst_ref=pair_buf.at[q // 2, r],
            send_sem=pair_send.at[q // 2, r], recv_sem=pair_recv.at[q // 2, r],
            device_id=(t, partner), device_id_type=MESH,
        )

    def rs_copy(c, slot, r):
        q = 2 * c + core
        return pltpu.make_async_remote_copy(
            src_ref=part.at[q * slab + r], dst_ref=rs_buf.at[slot, r],
            send_sem=rs_send.at[c, r], recv_sem=rs_recv.at[slot, r],
            device_id=(t, q), device_id_type=MESH,
        )

    def t_copy(d, source, target):
        return pltpu.make_async_remote_copy(
            src_ref=planes.at[pl.ds(p * slab, slab)], dst_ref=t_buf.at[source],
            send_sem=t_send.at[d], recv_sem=t_recv.at[d],
            device_id=(target, p), device_id_type=MESH,
        )

    def t_sends(act):
        for d in range(1, tn):
            target = t + d if d % 2 else t - d

            @pl.when((target >= 0) & (target < tn))
            def send():
                act(t_copy(d, t, target))

    def t_arrivals():
        for d in range(1, tn):
            source = t - d if d % 2 else t + d

            @pl.when((source >= 0) & (source < tn))
            def arrived():
                t_copy(d, source, t).wait_recv()

    def a_copy(s, target, r):
        return pltpu.make_async_remote_copy(
            src_ref=a_buf.at[s, r], dst_ref=a_buf.at[s, r],
            send_sem=a_send.at[s, target, r], recv_sem=a_recv.at[s, r],
            device_id=(target, p), device_id_type=MESH,
        )

    def a_route(r, act):
        for s in range(tn - 1):
            for target in range(s + 1, tn):
                if s % 2 == 0 or target == s + 1:

                    @pl.when(t == s)
                    def direct():
                        act(a_copy(s, target, r))

    def a_onward(r, act, wait):
        for s in range(1, tn - 2, 2):

            @pl.when(t == s + 1)
            def onward():
                if wait:
                    a_copy(s, s + 1, r).wait_recv()
                for target in range(s + 2, tn):
                    act(a_copy(s, target, r))

    def a_arrivals():
        for s in range(tn - 1):
            if s % 2 == 1 and s + 2 < tn:
                here = t > s + 1
            else:
                here = t > s

            @pl.when(here)
            def arrived():
                for r in range(slab):
                    a_copy(s, s + 1, r).wait_recv()

    def start(copy):
        copy.start()

    def sent(copy):
        copy.wait_send()

    def g_up(source, target):
        return pltpu.make_async_remote_copy(
            src_ref=g_col.at[source], dst_ref=g_col.at[source],
            send_sem=g_send.at[target], recv_sem=g_recv.at[source],
            device_id=(target, p), device_id_type=MESH,
        )

    def g_share(d):
        return pltpu.make_async_remote_copy(
            src_ref=g_col, dst_ref=g_buf.at[p],
            send_sem=share_send, recv_sem=share_recv,
            device_id=(t, lax.rem(p + d, pn)), device_id_type=MESH,
        )

    def g_shares():
        every = g_buf.at[pl.ds(0, pn - 1)]
        return pltpu.make_async_remote_copy(
            src_ref=every, dst_ref=every, send_sem=share_send, recv_sem=share_recv,
            device_id=(t, partner), device_id_type=MESH,
        )

    group_of = lax.broadcasted_iota(jnp.int32, (rows, lanes), 1) // length
    per_block = groups // occupied_ref.shape[0]
    lane_group = lax.broadcasted_iota(jnp.int32, (length, lanes), 1) // length
    occ = 0.25 + 0.75 * occupied_ref[0].astype(jnp.float32) * jnp.ones((length, lanes), jnp.float32)
    for i in range(1, occupied_ref.shape[0]):
        level = 0.25 + 0.75 * occupied_ref[i].astype(jnp.float32)
        occ = jnp.where(lane_group >= i * per_block, level, occ)

    at_group = [group_of == g for g in range(groups)]
    def pick(options):
        chosen = options[0]
        for g in range(1, groups):
            chosen = jnp.where(at_group[g], options[g], chosen)
        return chosen

    def turn(value, steps):
        steps = steps % groups
        return value if steps == 0 else pltpu.roll(value, steps * length, 1)

    plane_rows = length * rows

    weights_load.wait()
    psi_load(0).wait()
    for a in range(rows):
        plane_load(0, a).wait()

    @pl.loop(0, length // FORWARD)
    def forward(i):
        @pl.when(i == early // FORWARD)
        def rest():
            psi_load(1).wait()
            for a in range(rows):
                plane_load(1, a).wait()

        density = []
        for j in range(FORWARD):
            x = i * FORWARD + j
            for q in range(length // groups):
                v = planes[x, :, q * lanes : (q + 1) * lanes]
                turned = [turn(v, s) for s in range(groups)]
                for g in range(groups):
                    y = q * groups + g
                    spread = pick([turned[(h - g) % groups] for h in range(groups)])
                    density.append(spread * psi_ref[x, y : y + 1, :])
        waves = split_product(jnp.concatenate(density, axis=0), weights_ref[...])
        for j in range(FORWARD):
            wave = waves[j * plane_rows : (j + 1) * plane_rows]
            modes = flat_dft([wave[y * rows : (y + 1) * rows] for y in range(length)])
            for m in range(length):
                spec[i * FORWARD + j, m] = modes[m]

    t_buf[t] = planes[pl.ds(p * slab, slab)]
    for x in range(length):
        psi_ref[x] = psi_ref[x] * occ
    for s in range(1, tn):

        @pl.when(s > t)
        def clear():
            a_buf[s] = jnp.zeros(a_buf.shape[1:], jnp.float32)
            g_col[s] = jnp.zeros(g_col.shape[1:], jnp.float32)

    gram_ref[...] = jnp.zeros_like(gram_ref)
    table_load.wait()
    pl.semaphore_wait(barrier, tn + pn - 2)
    t_sends(start)

    @pl.loop(0, length)
    def middle(m):
        modes = flat_dft([spec[x, m] for x in range(length)])
        half = length // 2
        scaled = []
        for i in range(length):
            k = i if i <= half else i - half
            scaled.append(modes[i] * table_ref[m, k : k + 1, :])
        values = flat_dft_transposed(scaled)
        for x in range(length):
            spec[x, m] = values[x]

    per = chips // BACKWARD

    @pl.loop(0, 2 * slab * per)
    def backward(n):
        i = n // per
        first = lax.rem(n, per) * BACKWARD
        odd = lax.rem(i, 2)
        last = i == 2 * slab - 1
        away = (i == 0) | ((odd == 1) & jnp.logical_not(last))
        r = jnp.where(away, (i + 1) // 2, jnp.where(last, slab - 1, i // 2 - 1))
        side = jnp.where(away, 1 - core, core)
        owners = [2 * lax.rem(chip + 1 + first + j, chips) + side for j in range(BACKWARD)]
        values = []
        for q in owners:
            values += flat_dft_transposed([spec[q * slab + r, m] for m in range(length)])
        potentials = split_product(jnp.concatenate(values, axis=0), weights_ref[...])
        for j, owner in enumerate(owners):
            x = owner * slab + r
            potential = potentials[j * plane_rows : (j + 1) * plane_rows]
            for q in range(length // groups):
                terms = []
                for g in range(groups):
                    y = q * groups + g
                    terms.append(potential[y * rows : (y + 1) * rows] * psi_ref[x, y : y + 1, :])
                total = None
                for s in range(groups):
                    moved = turn(pick([terms[(h - s) % groups] for h in range(groups)]), -s)
                    total = moved if total is None else total + moved
                part[x, :, q * lanes : (q + 1) * lanes] = total

        @pl.when(away)
        def to_partner():
            for owner in owners:
                pair_copy(owner, r).start()

        @pl.when(jnp.logical_not(away))
        def to_owners():
            for j, owner in enumerate(owners):
                pair_copy(owner, r).wait_recv()

                @pl.when(first + j < chips - 1)
                def send():
                    x = owner * slab + r
                    part[x] = part[x] + pair_buf[owner // 2, r]
                    rs_copy(owner // 2, chip, r).start()

    t_arrivals()

    @pl.loop(0, slab)
    def reduce(r):
        own = part[p * slab + r] + pair_buf[chip, r]
        for d in range(1, chips):
            c = lax.rem(chip + d, chips)
            rs_copy(c, c, r).wait_recv()
            own = own + rs_buf[c, r]
        a_buf[t, r] = own

        @pl.when(r < slab - HELD)
        def at_once():
            a_route(r, start)

        every = jnp.concatenate([t_buf[s, r] for s in range(tn)], axis=0)
        gram_ref[...] += lax.dot_general(
            own, every, (((1,), (1,)), ((), ())),
            precision=HIGHEST, preferred_element_type=jnp.float32,
        )

    gram = gram_ref[...] * (1.0 / all_cells)
    fold = 128 // total_rows
    short = rows // fold
    g_col[t] = jnp.concatenate([gram[i * short : (i + 1) * short] for i in range(fold)], axis=1)
    for target in reversed(range(1, tn)):

        @pl.when(t < target)
        def upward():
            g_up(t, target).start()

    for r in range(slab - HELD):
        a_onward(r, start, True)
    for r in range(slab - HELD, slab):
        a_route(r, start)
    for s in range(tn - 1):

        @pl.when(t > s)
        def below():
            g_up(s, t).wait_recv()

    for d in range(1, pn):
        g_share(d).start()
    g_buf[p] = g_col[...]
    t_sends(sent)

    @pl.loop(0, slab)
    def drain(r):
        for c in range(chips):
            pair_copy(2 * c + 1 - core, r).wait_send()
        for d in range(1, chips):
            rs_copy(lax.rem(chip + d, chips), chip, r).wait_send()

    for r in range(slab - HELD, slab):
        a_onward(r, start, True)
    g_shares().wait_recv()
    blocks = []
    summed = g_buf[0]
    for q in range(1, pn):
        summed = summed + g_buf[q]
    for s in range(tn):
        blocks += [summed[s, :, i * total_rows : (i + 1) * total_rows] for i in range(fold)]
    square = jnp.concatenate(blocks, axis=0)
    square = jnp.concatenate(
        [square, jnp.zeros((total_rows, width - total_rows), jnp.float32)], axis=1
    )
    row_of = lax.broadcasted_iota(jnp.int32, (total_rows, width), 0)
    lane_of = lax.broadcasted_iota(jnp.int32, (total_rows, width), 1)
    row_block, lane_block = row_of // rows, lane_of // rows
    apart = lane_block - row_block
    odd = lax.rem(jnp.abs(apart), 2) == 1
    held = (apart == 0) | ((apart < 0) & odd) | ((apart > 0) & jnp.logical_not(odd))
    held = held & (row_block <= t) & (lane_block <= t)
    square = jnp.where(held, square, 0.0)
    padded = jnp.concatenate([square, jnp.zeros((width - total_rows, width), jnp.float32)], axis=0)
    both = square + jnp.transpose(padded)[:total_rows]
    symmetric = jnp.where(apart == 0, 0.5 * both, both)
    unit = (lane_of == row_of + total_rows) | ((lane_of == row_of) & (row_block > t))
    work = jnp.where(unit, 1.0, symmetric)
    scale = jnp.zeros((total_rows, width), jnp.float32)
    for k in range(0, total_rows, PIVOTS):
        columns = [
            jnp.broadcast_to(work[:, k + i : k + i + 1], (total_rows, width)) for i in range(PIVOTS)
        ]
        lines = [work[k + i : k + i + 1, :] for i in range(PIVOTS)]
        corner = [[columns[j][k + i : k + i + 1, :] for j in range(PIVOTS)] for i in range(PIVOTS)]
        for i in range(PIVOTS):
            pivot = corner[i][i]
            scale = jnp.where(row_of == k + i, 1.0 / jnp.sqrt(pivot), scale)
            inverse = 1.0 / pivot
            scaled = lines[i] * inverse
            for m in range(i + 1, PIVOTS):
                factor = corner[i][m] * inverse
                columns[m] = columns[m] - columns[i] * factor
                lines[m] = lines[m] - corner[m][i] * scaled
                for h in range(i + 1, PIVOTS):
                    corner[h][m] = corner[h][m] - corner[h][i] * factor
            work = work - jnp.where(row_of > k + i, columns[i], 0.0) * scaled
    keeping = (row_of < retained_ref[0]).astype(jnp.float32)
    inv_ref[...] = work * scale * keeping
    mine = inv_ref[pl.ds(pl.multiple_of(t * rows, rows), rows), :][:, total_rows : 2 * total_rows]
    a_arrivals()
    for x in range(slab):
        every = jnp.concatenate([a_buf[s, x] for s in range(tn)], axis=0)
        out_ref[:, x, :] = jnp.dot(
            mine, every, precision=HIGHEST, preferred_element_type=jnp.float32
        )

    for target in range(1, tn):

        @pl.when(t < target)
        def ended():
            g_up(t, target).wait_send()

    g_shares().wait_send()
    for r in range(slab):
        a_route(r, sent)
        a_onward(r, sent, False)


def constants(length, groups):
    i = np.arange(length)
    phase = 2.0 * np.pi / length * (i[:, None] * i[None, :] % length)
    cas = np.kron(np.eye(groups), np.cos(phase) + np.sin(phase)).astype(np.float32)
    high = cas.astype(jnp.bfloat16)
    low = (cas - high.astype(np.float32)).astype(jnp.bfloat16)
    weights = np.concatenate([np.concatenate([high, low], 1)] * 2, 0)
    signed = np.where(i < length // 2, i, i - length)
    half = length // 2
    k = np.arange(half + 1)
    wave = (2.0 * np.pi / length) ** 2
    total = wave * ((k**2)[:, None, None] + (k**2)[None, :, None] + (signed**2)[None, None, :])
    coulomb = np.where(total > 0, 4 * np.pi / np.where(total > 0, total, 1.0), 0.0)
    fold = np.where((k == 0) | (k == half), 1.0, 2.0)
    coulomb = coulomb * fold[:, None, None] * fold[None, :, None] / length**3
    order = np.concatenate([np.arange(half + 1), np.arange(1, half)])
    table = np.tile(coulomb[order], (1, 1, groups)).astype(np.float32)
    return weights, table


def shards(tn, pn, targets, partners, occupied, retained):
    rows, length, cells = targets.shape
    lanes = partners.shape[2]
    groups = lanes // length
    slab = length // pn
    weights, table = constants(length, groups)
    total_rows = tn * rows
    width = -(-2 * total_rows // 128) * 128
    vmem = pl.BlockSpec(memory_space=pltpu.VMEM)
    smem = pl.BlockSpec(memory_space=pltpu.SMEM)
    hbm = pl.BlockSpec(memory_space=pl.ANY)
    planes = pltpu.VMEM((length, rows, cells), jnp.float32)
    block = pltpu.VMEM((tn, slab, rows, cells), jnp.float32)
    received = pltpu.VMEM((pn // 2, slab, rows, cells), jnp.float32)
    return pl.pallas_call(
        functools.partial(kernel, tn, pn),
        out_shape=pltpu.VMEM((rows, slab, cells), jnp.float32),
        in_specs=[hbm, hbm, hbm, hbm, smem, smem],
        out_specs=vmem,
        scratch_shapes=[
            planes,
            pltpu.VMEM(partners.shape, jnp.float32),
            pltpu.VMEM(weights.shape, weights.dtype),
            pltpu.VMEM(table.shape, jnp.float32),
            pltpu.VMEM((length, length + 1, rows, lanes), jnp.float32),
            planes,
            received,
            received,
            block,
            block,
            pltpu.VMEM((rows, total_rows), jnp.float32),
            pltpu.VMEM((tn, rows * total_rows // 128, 128), jnp.float32),
            pltpu.VMEM((pn, tn, rows * total_rows // 128, 128), jnp.float32),
            pltpu.VMEM((total_rows, width), jnp.float32),
        ],
        compiler_params=pltpu.CompilerParams(collective_id=0, has_side_effects=True),
        name="exchange",
    )(targets, partners, jnp.asarray(weights), jnp.asarray(table), occupied, retained)


def solution(mesh):
    return jax.shard_map(
        functools.partial(shards, mesh.shape["tgt"], mesh.shape["ptr"]),
        mesh=mesh,
        in_specs=(P("tgt", None, None), P(None, None, "ptr"), P("ptr"), P()),
        out_specs=P("tgt", "ptr", None),
        check_vma=False,
    )
```

```python
import functools
import math

import jax
import jax.numpy as jnp
import numpy as np
from jax import lax
from jax.experimental import pallas as pl
from jax.experimental.pallas import tpu as pltpu
from jax.sharding import PartitionSpec as P

HIGHEST = lax.Precision.HIGHEST
MESH = pl.DeviceIdType.MESH
FORWARD = 8
BACKWARD = 4
PIVOTS = 8
MIDDLE = 2
HELD = 2


def turned_by(n, k, re, im):
    c, s = math.cos(2 * math.pi * k / n), math.sin(2 * math.pi * k / n)
    return c * re + s * im, c * im - s * re


def real_dft(values):
    n = len(values)
    if n == 1:
        return [values[0]], [None]
    if n == 2:
        return [values[0] + values[1], values[0] - values[1]], [None, None]
    half, quarter, eighth = n // 2, n // 4, n // 8
    even_re, even_im = real_dft(values[0::2])
    one_re, one_im = real_dft(values[1::4])
    three_re, three_im = real_dft(values[3::4])
    re, im = [None] * (half + 1), [None] * (half + 1)
    total = one_re[0] + three_re[0]
    re[0], re[half] = even_re[0] + total, even_re[0] - total
    re[quarter], im[quarter] = even_re[quarter], three_re[0] - one_re[0]
    for k in range(1, eighth + 1):
        if 2 * k == quarter:
            c = math.sqrt(0.5)
            a, b = c * (one_re[k] - three_re[k]), c * (one_re[k] + three_re[k])
            re[k], re[half - k] = even_re[k] + a, even_re[k] - a
            im[k], im[half - k] = even_im[k] - b, -b - even_im[k]
            continue
        one = turned_by(n, k, one_re[k], one_im[k])
        three = turned_by(n, 3 * k, three_re[k], three_im[k])
        sum_re, sum_im = one[0] + three[0], one[1] + three[1]
        gap_re, gap_im = one[0] - three[0], one[1] - three[1]
        re[k], re[half - k] = even_re[k] + sum_re, even_re[k] - sum_re
        im[k], im[half - k] = even_im[k] + sum_im, sum_im - even_im[k]
        mirror = quarter - k
        re[quarter + k], re[mirror] = even_re[mirror] + gap_im, even_re[mirror] - gap_im
        im[quarter + k], im[mirror] = -gap_re - even_im[mirror], even_im[mirror] - gap_re
    return re, im


def real_dft_transposed(re, im):
    half = len(re) - 1
    if half == 0:
        return [re[0]]
    if half == 1:
        return [re[0] + re[1], re[0] - re[1]]
    n = 2 * half
    quarter, eighth = half // 2, half // 4
    even_re, even_im = [None] * (quarter + 1), [None] * (quarter + 1)
    one_re, one_im = [None] * (eighth + 1), [None] * (eighth + 1)
    three_re, three_im = [None] * (eighth + 1), [None] * (eighth + 1)
    even_re[0], total = re[0] + re[half], re[0] - re[half]
    even_re[quarter] = re[quarter]
    one_re[0], three_re[0] = total - im[quarter], total + im[quarter]
    for k in range(1, eighth + 1):
        sum_re, even_re[k] = re[k] - re[half - k], re[k] + re[half - k]
        sum_im, even_im[k] = im[k] + im[half - k], im[k] - im[half - k]
        if 2 * k == quarter:
            c = math.sqrt(0.5)
            one_re[k], three_re[k] = c * (sum_re - sum_im), -c * (sum_re + sum_im)
            continue
        mirror = quarter - k
        even_re[mirror], gap_im = re[quarter + k] + re[mirror], re[quarter + k] - re[mirror]
        even_im[mirror] = im[mirror] - im[quarter + k]
        gap_re = -(im[quarter + k] + im[mirror])
        one = sum_re + gap_re, sum_im + gap_im
        three = sum_re - gap_re, sum_im - gap_im
        one_re[k], one_im[k] = turned_by(n, -k, *one)
        three_re[k], three_im[k] = turned_by(n, -3 * k, *three)
    values = [None] * n
    values[0::2] = real_dft_transposed(even_re, even_im)
    values[1::4] = real_dft_transposed(one_re, one_im)
    values[3::4] = real_dft_transposed(three_re, three_im)
    return values


def flat_dft(values):
    re, im = real_dft(values)
    return re + im[1:-1]


def flat_dft_transposed(modes):
    half = len(modes) // 2
    return real_dft_transposed(modes[: half + 1], [None] + modes[half + 1 :] + [None])


def split_product(field, weights):
    width = field.shape[1]
    high = field.astype(jnp.bfloat16)
    low = (field - high.astype(jnp.float32)).astype(jnp.bfloat16)
    both = jnp.dot(
        jnp.concatenate([high, low], axis=1), weights, preferred_element_type=jnp.float32
    )
    return both[:, :width] + both[:, width:]


def kernel(
    tn, pn, t_hbm, psi_hbm, weights_hbm, table_hbm, occupied_ref, retained_ref, out_ref,
    planes, psi_ref, weights_ref, table_ref, spec, part, pair_buf, rs_buf, t_buf, a_buf,
    gram_ref, g_col, g_buf, inv_ref,
):
    slab = planes.shape[0] // pn
    rows = planes.shape[1]
    dma = pltpu.SemaphoreType.DMA
    pl.run_scoped(
        functools.partial(
            exchange, tn, pn, t_hbm, psi_hbm, weights_hbm, table_hbm, occupied_ref, retained_ref,
            out_ref, planes, psi_ref, weights_ref, table_ref, spec, part, pair_buf, rs_buf, t_buf,
            a_buf, gram_ref, g_col, g_buf, inv_ref,
        ),
        dma((2, rows)), dma((4,)), dma((pn // 2, slab)), dma((pn // 2, slab)),
        dma((pn // 2, slab)), dma((pn // 2, slab)), dma((tn,)), dma((tn,)),
        dma((tn, tn, slab)), dma((tn, slab)), dma((tn,)), dma((tn,)), dma, dma,
    )


def exchange(
    tn, pn, t_hbm, psi_hbm, weights_hbm, table_hbm, occupied_ref, retained_ref, out_ref,
    planes, psi_ref, weights_ref, table_ref, spec, part, pair_buf, rs_buf, t_buf, a_buf,
    gram_ref, g_col, g_buf, inv_ref,
    plane_sem, load_sem, pair_send, pair_recv, rs_send, rs_recv, t_send, t_recv,
    a_send, a_recv, g_send, g_recv, share_send, share_recv,
):
    t, p = lax.axis_index("tgt"), lax.axis_index("ptr")
    length, rows, cells = planes.shape
    lanes = psi_ref.shape[2]
    groups = lanes // length
    slab = length // pn
    all_cells = length * cells
    total_rows = tn * rows
    width = inv_ref.shape[1]
    chips = pn // 2
    chip, core = p // 2, lax.rem(p, 2)
    partner = p + 1 - 2 * core
    early = length // 4

    def plane_load(c, a):
        xs = pl.ds(0, early) if c == 0 else pl.ds(early, length - early)
        return pltpu.make_async_copy(t_hbm.at[a, xs, :], planes.at[xs, a, :], plane_sem.at[c, a])

    def psi_load(c):
        xs = pl.ds(0, early) if c == 0 else pl.ds(early, length - early)
        return pltpu.make_async_copy(psi_hbm.at[xs], psi_ref.at[xs], load_sem.at[c])

    weights_load = pltpu.make_async_copy(weights_hbm, weights_ref, load_sem.at[2])
    table_load = pltpu.make_async_copy(table_hbm, table_ref, load_sem.at[3])

    weights_load.start()
    for c in range(2):
        psi_load(c).start()
        for a in range(rows):
            plane_load(c, a).start()
    table_load.start()

    barrier = pltpu.get_barrier_semaphore()
    for tt in range(tn):

        @pl.when(t != tt)
        def column():
            pl.semaphore_signal(barrier, inc=1, device_id=(tt, p), device_id_type=MESH)

    for d in range(1, pn):
        pl.semaphore_signal(
            barrier, inc=1, device_id=(t, lax.rem(p + d, pn)), device_id_type=MESH
        )

    def pair_copy(q, r):
        return pltpu.make_async_remote_copy(
            src_ref=part.at[q * slab + r], dst_ref=pair_buf.at[q // 2, r],
            send_sem=pair_send.at[q // 2, r], recv_sem=pair_recv.at[q // 2, r],
            device_id=(t, partner), device_id_type=MESH,
        )

    def rs_copy(c, slot, r):
        q = 2 * c + core
        return pltpu.make_async_remote_copy(
            src_ref=part.at[q * slab + r], dst_ref=rs_buf.at[slot, r],
            send_sem=rs_send.at[c, r], recv_sem=rs_recv.at[slot, r],
            device_id=(t, q), device_id_type=MESH,
        )

    def t_copy(d, source, target):
        return pltpu.make_async_remote_copy(
            src_ref=planes.at[pl.ds(p * slab, slab)], dst_ref=t_buf.at[source],
            send_sem=t_send.at[d], recv_sem=t_recv.at[d],
            device_id=(target, p), device_id_type=MESH,
        )

    def t_sends(act):
        for d in range(1, tn):
            target = t + d if d % 2 else t - d

            @pl.when((target >= 0) & (target < tn))
            def send():
                act(t_copy(d, t, target))

    def t_arrivals():
        for d in range(1, tn):
            source = t - d if d % 2 else t + d

            @pl.when((source >= 0) & (source < tn))
            def arrived():
                t_copy(d, source, t).wait_recv()

    def a_copy(s, target, r):
        return pltpu.make_async_remote_copy(
            src_ref=a_buf.at[s, r], dst_ref=a_buf.at[s, r],
            send_sem=a_send.at[s, target, r], recv_sem=a_recv.at[s, r],
            device_id=(target, p), device_id_type=MESH,
        )

    def a_route(r, act):
        for s in range(tn - 1):
            for target in range(s + 1, tn):
                if s % 2 == 0 or target == s + 1:

                    @pl.when(t == s)
                    def direct():
                        act(a_copy(s, target, r))

    def a_onward(r, act, wait):
        for s in range(1, tn - 2, 2):

            @pl.when(t == s + 1)
            def onward():
                if wait:
                    a_copy(s, s + 1, r).wait_recv()
                for target in range(s + 2, tn):
                    act(a_copy(s, target, r))

    def a_arrivals(r):
        for s in range(tn - 1):
            if s % 2 == 1 and s + 2 < tn:
                here = t > s + 1
            else:
                here = t > s

            @pl.when(here)
            def arrived():
                a_copy(s, s + 1, r).wait_recv()

    def start(copy):
        copy.start()

    def sent(copy):
        copy.wait_send()

    def g_up(source, target):
        return pltpu.make_async_remote_copy(
            src_ref=g_col.at[source], dst_ref=g_col.at[source],
            send_sem=g_send.at[target], recv_sem=g_recv.at[source],
            device_id=(target, p), device_id_type=MESH,
        )

    def g_share(d):
        return pltpu.make_async_remote_copy(
            src_ref=g_col, dst_ref=g_buf.at[p],
            send_sem=share_send, recv_sem=share_recv,
            device_id=(t, lax.rem(p + d, pn)), device_id_type=MESH,
        )

    def g_shares():
        every = g_buf.at[pl.ds(0, pn - 1)]
        return pltpu.make_async_remote_copy(
            src_ref=every, dst_ref=every, send_sem=share_send, recv_sem=share_recv,
            device_id=(t, partner), device_id_type=MESH,
        )

    group_of = lax.broadcasted_iota(jnp.int32, (rows, lanes), 1) // length
    per_block = groups // occupied_ref.shape[0]
    lane_group = lax.broadcasted_iota(jnp.int32, (length, lanes), 1) // length
    occ = 0.25 + 0.75 * occupied_ref[0].astype(jnp.float32) * jnp.ones((length, lanes), jnp.float32)
    for i in range(1, occupied_ref.shape[0]):
        level = 0.25 + 0.75 * occupied_ref[i].astype(jnp.float32)
        occ = jnp.where(lane_group >= i * per_block, level, occ)

    at_group = [group_of == g for g in range(groups)]
    def pick(options):
        chosen = options[0]
        for g in range(1, groups):
            chosen = jnp.where(at_group[g], options[g], chosen)
        return chosen

    def turn(value, steps):
        steps = steps % groups
        return value if steps == 0 else pltpu.roll(value, steps * length, 1)

    plane_rows = length * rows

    weights_load.wait()
    psi_load(0).wait()
    for a in range(rows):
        plane_load(0, a).wait()

    @pl.loop(0, length // FORWARD)
    def forward(i):
        @pl.when(i == early // FORWARD)
        def rest():
            psi_load(1).wait()
            for a in range(rows):
                plane_load(1, a).wait()

        density = []
        for j in range(FORWARD):
            x = i * FORWARD + j
            for q in range(length // groups):
                v = planes[x, :, q * lanes : (q + 1) * lanes]
                turned = [turn(v, s) for s in range(groups)]
                for g in range(groups):
                    y = q * groups + g
                    spread = pick([turned[(h - g) % groups] for h in range(groups)])
                    density.append(spread * psi_ref[x, y : y + 1, :])
        waves = split_product(jnp.concatenate(density, axis=0), weights_ref[...])
        for j in range(FORWARD):
            wave = waves[j * plane_rows : (j + 1) * plane_rows]
            modes = flat_dft([wave[y * rows : (y + 1) * rows] for y in range(length)])
            for m in range(length):
                spec[i * FORWARD + j, m] = modes[m]

    t_buf[t] = planes[pl.ds(p * slab, slab)]
    for x in range(length):
        psi_ref[x] = psi_ref[x] * occ
    for s in range(1, tn):

        @pl.when(s > t)
        def clear():
            a_buf[s] = jnp.zeros(a_buf.shape[1:], jnp.float32)
            g_col[s] = jnp.zeros(g_col.shape[1:], jnp.float32)

    gram_ref[...] = jnp.zeros_like(gram_ref)
    table_load.wait()
    pl.semaphore_wait(barrier, tn + pn - 2)
    t_sends(start)

    @pl.loop(0, length // MIDDLE)
    def middle(step):
        half = length // 2
        for j in range(MIDDLE):
            m = step * MIDDLE + j
            modes = flat_dft([spec[x, m] for x in range(length)])
            scaled = []
            for i in range(length):
                k = i if i <= half else i - half
                scaled.append(modes[i] * table_ref[m, k : k + 1, :])
            values = flat_dft_transposed(scaled)
            for x in range(length):
                spec[x, m] = values[x]

    per = chips // BACKWARD

    @pl.loop(0, 2 * slab * per)
    def backward(n):
        i = n // per
        first = lax.rem(n, per) * BACKWARD
        odd = lax.rem(i, 2)
        last = i == 2 * slab - 1
        away = (i == 0) | ((odd == 1) & jnp.logical_not(last))
        r = jnp.where(away, (i + 1) // 2, jnp.where(last, slab - 1, i // 2 - 1))
        side = jnp.where(away, 1 - core, core)
        owners = [2 * lax.rem(chip + 1 + first + j, chips) + side for j in range(BACKWARD)]
        values = []
        for q in owners:
            values += flat_dft_transposed([spec[q * slab + r, m] for m in range(length)])
        potentials = split_product(jnp.concatenate(values, axis=0), weights_ref[...])
        for j, owner in enumerate(owners):
            x = owner * slab + r
            potential = potentials[j * plane_rows : (j + 1) * plane_rows]
            for q in range(length // groups):
                terms = []
                for g in range(groups):
                    y = q * groups + g
                    terms.append(potential[y * rows : (y + 1) * rows] * psi_ref[x, y : y + 1, :])
                total = None
                for s in range(groups):
                    moved = turn(pick([terms[(h - s) % groups] for h in range(groups)]), -s)
                    total = moved if total is None else total + moved
                part[x, :, q * lanes : (q + 1) * lanes] = total

        @pl.when(away)
        def to_partner():
            for owner in owners:
                pair_copy(owner, r).start()

        @pl.when(jnp.logical_not(away))
        def to_owners():
            for j, owner in enumerate(owners):
                pair_copy(owner, r).wait_recv()

                @pl.when(first + j < chips - 1)
                def send():
                    x = owner * slab + r
                    part[x] = part[x] + pair_buf[owner // 2, r]
                    rs_copy(owner // 2, chip, r).start()

    def add_gram(r):
        every = jnp.concatenate([t_buf[s, r] for s in range(tn)], axis=0)
        gram_ref[...] += lax.dot_general(
            a_buf[t, r], every, (((1,), (1,)), ((), ())),
            precision=HIGHEST, preferred_element_type=jnp.float32,
        )

    @pl.loop(0, slab)
    def reduce(r):
        own = part[p * slab + r] + pair_buf[chip, r]
        for d in range(1, chips):
            c = lax.rem(chip + d, chips)
            rs_copy(c, c, r).wait_recv()
            own = own + rs_buf[c, r]
        a_buf[t, r] = own

        @pl.when(r < slab - HELD)
        def at_once():
            a_route(r, start)

        @pl.when(r == 1)
        def met():
            t_arrivals()

        @pl.when(r > 0)
        def earlier():
            add_gram(r - 1)

    add_gram(slab - 1)
    gram = gram_ref[...] * (1.0 / all_cells)
    fold = 128 // total_rows
    short = rows // fold
    g_col[t] = jnp.concatenate([gram[i * short : (i + 1) * short] for i in range(fold)], axis=1)
    for target in reversed(range(1, tn)):

        @pl.when(t < target)
        def upward():
            g_up(t, target).start()

    for r in range(slab - HELD):
        a_onward(r, start, True)
    for r in range(slab - HELD, slab):
        a_route(r, start)
    for s in range(tn - 1):

        @pl.when(t > s)
        def below():
            g_up(s, t).wait_recv()

    for d in range(1, pn):
        g_share(d).start()
    g_buf[p] = g_col[...]
    t_sends(sent)

    @pl.loop(0, slab)
    def drain(r):
        for c in range(chips):
            pair_copy(2 * c + 1 - core, r).wait_send()
        for d in range(1, chips):
            rs_copy(lax.rem(chip + d, chips), chip, r).wait_send()

    for r in range(slab - HELD, slab):
        a_onward(r, start, True)
    g_shares().wait_recv()
    blocks = []
    summed = g_buf[0]
    for q in range(1, pn):
        summed = summed + g_buf[q]
    for s in range(tn):
        blocks += [summed[s, :, i * total_rows : (i + 1) * total_rows] for i in range(fold)]
    square = jnp.concatenate(blocks, axis=0)
    square = jnp.concatenate(
        [square, jnp.zeros((total_rows, width - total_rows), jnp.float32)], axis=1
    )
    row_of = lax.broadcasted_iota(jnp.int32, (total_rows, width), 0)
    lane_of = lax.broadcasted_iota(jnp.int32, (total_rows, width), 1)
    row_block, lane_block = row_of // rows, lane_of // rows
    apart = lane_block - row_block
    odd = lax.rem(jnp.abs(apart), 2) == 1
    held = (apart == 0) | ((apart < 0) & odd) | ((apart > 0) & jnp.logical_not(odd))
    held = held & (row_block <= t) & (lane_block <= t)
    square = jnp.where(held, square, 0.0)
    padded = jnp.concatenate([square, jnp.zeros((width - total_rows, width), jnp.float32)], axis=0)
    both = square + jnp.transpose(padded)[:total_rows]
    symmetric = jnp.where(apart == 0, 0.5 * both, both)
    unit = (lane_of == row_of + total_rows) | ((lane_of == row_of) & (row_block > t))
    work = jnp.where(unit, 1.0, symmetric)
    scale = jnp.zeros((total_rows, width), jnp.float32)
    for k in range(0, total_rows, PIVOTS):
        columns = [
            jnp.broadcast_to(work[:, k + i : k + i + 1], (total_rows, width)) for i in range(PIVOTS)
        ]
        lines = [work[k + i : k + i + 1, :] for i in range(PIVOTS)]
        corner = [[columns[j][k + i : k + i + 1, :] for j in range(PIVOTS)] for i in range(PIVOTS)]
        for i in range(PIVOTS):
            pivot = corner[i][i]
            scale = jnp.where(row_of == k + i, 1.0 / jnp.sqrt(pivot), scale)
            inverse = 1.0 / pivot
            scaled = lines[i] * inverse
            for m in range(i + 1, PIVOTS):
                factor = corner[i][m] * inverse
                columns[m] = columns[m] - columns[i] * factor
                lines[m] = lines[m] - corner[m][i] * scaled
                for h in range(i + 1, PIVOTS):
                    corner[h][m] = corner[h][m] - corner[h][i] * factor
            work = work - jnp.where(row_of > k + i, columns[i], 0.0) * scaled
    keeping = (row_of < retained_ref[0]).astype(jnp.float32)
    inv_ref[...] = work * scale * keeping
    mine = inv_ref[pl.ds(pl.multiple_of(t * rows, rows), rows), :][:, total_rows : 2 * total_rows]
    for x in range(slab):
        a_arrivals(x)
        every = jnp.concatenate([a_buf[s, x] for s in range(tn)], axis=0)
        out_ref[:, x, :] = jnp.dot(
            mine, every, precision=HIGHEST, preferred_element_type=jnp.float32
        )

    for target in range(1, tn):

        @pl.when(t < target)
        def ended():
            g_up(t, target).wait_send()

    g_shares().wait_send()
    for r in range(slab):
        a_route(r, sent)
        a_onward(r, sent, False)


def constants(length, groups):
    i = np.arange(length)
    phase = 2.0 * np.pi / length * (i[:, None] * i[None, :] % length)
    cas = np.kron(np.eye(groups), np.cos(phase) + np.sin(phase)).astype(np.float32)
    high = cas.astype(jnp.bfloat16)
    low = (cas - high.astype(np.float32)).astype(jnp.bfloat16)
    weights = np.concatenate([np.concatenate([high, low], 1)] * 2, 0)
    signed = np.where(i < length // 2, i, i - length)
    half = length // 2
    k = np.arange(half + 1)
    wave = (2.0 * np.pi / length) ** 2
    total = wave * ((k**2)[:, None, None] + (k**2)[None, :, None] + (signed**2)[None, None, :])
    coulomb = np.where(total > 0, 4 * np.pi / np.where(total > 0, total, 1.0), 0.0)
    fold = np.where((k == 0) | (k == half), 1.0, 2.0)
    coulomb = coulomb * fold[:, None, None] * fold[None, :, None] / length**3
    order = np.concatenate([np.arange(half + 1), np.arange(1, half)])
    table = np.tile(coulomb[order], (1, 1, groups)).astype(np.float32)
    return weights, table


def shards(tn, pn, targets, partners, occupied, retained):
    rows, length, cells = targets.shape
    lanes = partners.shape[2]
    groups = lanes // length
    slab = length // pn
    weights, table = constants(length, groups)
    total_rows = tn * rows
    width = -(-2 * total_rows // 128) * 128
    vmem = pl.BlockSpec(memory_space=pltpu.VMEM)
    smem = pl.BlockSpec(memory_space=pltpu.SMEM)
    hbm = pl.BlockSpec(memory_space=pl.ANY)
    planes = pltpu.VMEM((length, rows, cells), jnp.float32)
    block = pltpu.VMEM((tn, slab, rows, cells), jnp.float32)
    received = pltpu.VMEM((pn // 2, slab, rows, cells), jnp.float32)
    return pl.pallas_call(
        functools.partial(kernel, tn, pn),
        out_shape=pltpu.VMEM((rows, slab, cells), jnp.float32),
        in_specs=[hbm, hbm, hbm, hbm, smem, smem],
        out_specs=vmem,
        scratch_shapes=[
            planes,
            pltpu.VMEM(partners.shape, jnp.float32),
            pltpu.VMEM(weights.shape, weights.dtype),
            pltpu.VMEM(table.shape, jnp.float32),
            pltpu.VMEM((length, length + 1, rows, lanes), jnp.float32),
            planes,
            received,
            received,
            block,
            block,
            pltpu.VMEM((rows, total_rows), jnp.float32),
            pltpu.VMEM((tn, rows * total_rows // 128, 128), jnp.float32),
            pltpu.VMEM((pn, tn, rows * total_rows // 128, 128), jnp.float32),
            pltpu.VMEM((total_rows, width), jnp.float32),
        ],
        compiler_params=pltpu.CompilerParams(collective_id=0, has_side_effects=True),
        name="exchange",
    )(targets, partners, jnp.asarray(weights), jnp.asarray(table), occupied, retained)


def solution(mesh):
    return jax.shard_map(
        functools.partial(shards, mesh.shape["tgt"], mesh.shape["ptr"]),
        mesh=mesh,
        in_specs=(P("tgt", None, None), P(None, None, "ptr"), P("ptr"), P()),
        out_specs=P("tgt", "ptr", None),
        check_vma=False,
    )
```

```python
import functools
import math

import jax
import jax.numpy as jnp
import numpy as np
from jax import lax
from jax.experimental import pallas as pl
from jax.experimental.pallas import tpu as pltpu
from jax.sharding import PartitionSpec as P

HIGHEST = lax.Precision.HIGHEST
MESH = pl.DeviceIdType.MESH
FORWARD = 8
BACKWARD = 4
PIVOTS = 8
MIDDLE = 2
HELD = 2


def turned_by(n, k, re, im):
    c, s = math.cos(2 * math.pi * k / n), math.sin(2 * math.pi * k / n)
    return c * re + s * im, c * im - s * re


def real_dft(values):
    n = len(values)
    if n == 1:
        return [values[0]], [None]
    if n == 2:
        return [values[0] + values[1], values[0] - values[1]], [None, None]
    half, quarter, eighth = n // 2, n // 4, n // 8
    even_re, even_im = real_dft(values[0::2])
    one_re, one_im = real_dft(values[1::4])
    three_re, three_im = real_dft(values[3::4])
    re, im = [None] * (half + 1), [None] * (half + 1)
    total = one_re[0] + three_re[0]
    re[0], re[half] = even_re[0] + total, even_re[0] - total
    re[quarter], im[quarter] = even_re[quarter], three_re[0] - one_re[0]
    for k in range(1, eighth + 1):
        if 2 * k == quarter:
            c = math.sqrt(0.5)
            a, b = c * (one_re[k] - three_re[k]), c * (one_re[k] + three_re[k])
            re[k], re[half - k] = even_re[k] + a, even_re[k] - a
            im[k], im[half - k] = even_im[k] - b, -b - even_im[k]
            continue
        one = turned_by(n, k, one_re[k], one_im[k])
        three = turned_by(n, 3 * k, three_re[k], three_im[k])
        sum_re, sum_im = one[0] + three[0], one[1] + three[1]
        gap_re, gap_im = one[0] - three[0], one[1] - three[1]
        re[k], re[half - k] = even_re[k] + sum_re, even_re[k] - sum_re
        im[k], im[half - k] = even_im[k] + sum_im, sum_im - even_im[k]
        mirror = quarter - k
        re[quarter + k], re[mirror] = even_re[mirror] + gap_im, even_re[mirror] - gap_im
        im[quarter + k], im[mirror] = -gap_re - even_im[mirror], even_im[mirror] - gap_re
    return re, im


def real_dft_transposed(re, im):
    half = len(re) - 1
    if half == 0:
        return [re[0]]
    if half == 1:
        return [re[0] + re[1], re[0] - re[1]]
    n = 2 * half
    quarter, eighth = half // 2, half // 4
    even_re, even_im = [None] * (quarter + 1), [None] * (quarter + 1)
    one_re, one_im = [None] * (eighth + 1), [None] * (eighth + 1)
    three_re, three_im = [None] * (eighth + 1), [None] * (eighth + 1)
    even_re[0], total = re[0] + re[half], re[0] - re[half]
    even_re[quarter] = re[quarter]
    one_re[0], three_re[0] = total - im[quarter], total + im[quarter]
    for k in range(1, eighth + 1):
        sum_re, even_re[k] = re[k] - re[half - k], re[k] + re[half - k]
        sum_im, even_im[k] = im[k] + im[half - k], im[k] - im[half - k]
        if 2 * k == quarter:
            c = math.sqrt(0.5)
            one_re[k], three_re[k] = c * (sum_re - sum_im), -c * (sum_re + sum_im)
            continue
        mirror = quarter - k
        even_re[mirror], gap_im = re[quarter + k] + re[mirror], re[quarter + k] - re[mirror]
        even_im[mirror] = im[mirror] - im[quarter + k]
        gap_re = -(im[quarter + k] + im[mirror])
        one = sum_re + gap_re, sum_im + gap_im
        three = sum_re - gap_re, sum_im - gap_im
        one_re[k], one_im[k] = turned_by(n, -k, *one)
        three_re[k], three_im[k] = turned_by(n, -3 * k, *three)
    values = [None] * n
    values[0::2] = real_dft_transposed(even_re, even_im)
    values[1::4] = real_dft_transposed(one_re, one_im)
    values[3::4] = real_dft_transposed(three_re, three_im)
    return values


def flat_dft(values):
    re, im = real_dft(values)
    return re + im[1:-1]


def flat_dft_transposed(modes):
    half = len(modes) // 2
    return real_dft_transposed(modes[: half + 1], [None] + modes[half + 1 :] + [None])


def split_product(field, weights):
    width = field.shape[1]
    high = field.astype(jnp.bfloat16)
    low = (field - high.astype(jnp.float32)).astype(jnp.bfloat16)
    both = jnp.dot(
        jnp.concatenate([high, low], axis=1), weights, preferred_element_type=jnp.float32
    )
    return both[:, :width] + both[:, width:]


def kernel(
    tn, pn, t_hbm, psi_hbm, weights_hbm, table_hbm, occupied_ref, retained_ref, out_ref,
    planes, psi_ref, weights_ref, table_ref, spec, part, pair_buf, rs_buf, t_buf, a_buf,
    gram_ref, g_col, g_buf, inv_ref,
):
    slab = planes.shape[0] // pn
    rows = planes.shape[1]
    dma = pltpu.SemaphoreType.DMA
    pl.run_scoped(
        functools.partial(
            exchange, tn, pn, t_hbm, psi_hbm, weights_hbm, table_hbm, occupied_ref, retained_ref,
            out_ref, planes, psi_ref, weights_ref, table_ref, spec, part, pair_buf, rs_buf, t_buf,
            a_buf, gram_ref, g_col, g_buf, inv_ref,
        ),
        dma((2, rows)), dma((4,)), dma((pn // 2, slab)), dma((pn // 2, slab)),
        dma((pn // 2, slab)), dma((pn // 2, slab)), dma((tn,)), dma((tn,)),
        dma((tn, tn, slab)), dma((tn, slab)), dma((tn,)), dma((tn,)), dma, dma,
    )


def exchange(
    tn, pn, t_hbm, psi_hbm, weights_hbm, table_hbm, occupied_ref, retained_ref, out_ref,
    planes, psi_ref, weights_ref, table_ref, spec, part, pair_buf, rs_buf, t_buf, a_buf,
    gram_ref, g_col, g_buf, inv_ref,
    plane_sem, load_sem, pair_send, pair_recv, rs_send, rs_recv, t_send, t_recv,
    a_send, a_recv, g_send, g_recv, share_send, share_recv,
):
    t, p = lax.axis_index("tgt"), lax.axis_index("ptr")
    length, rows, cells = planes.shape
    lanes = psi_ref.shape[2]
    groups = lanes // length
    slab = length // pn
    all_cells = length * cells
    total_rows = tn * rows
    width = inv_ref.shape[1]
    chips = pn // 2
    chip, core = p // 2, lax.rem(p, 2)
    partner = p + 1 - 2 * core
    early = length // 4

    def plane_load(c, a):
        xs = pl.ds(0, early) if c == 0 else pl.ds(early, length - early)
        return pltpu.make_async_copy(t_hbm.at[a, xs, :], planes.at[xs, a, :], plane_sem.at[c, a])

    def psi_load(c):
        xs = pl.ds(0, early) if c == 0 else pl.ds(early, length - early)
        return pltpu.make_async_copy(psi_hbm.at[xs], psi_ref.at[xs], load_sem.at[c])

    weights_load = pltpu.make_async_copy(weights_hbm, weights_ref, load_sem.at[2])
    table_load = pltpu.make_async_copy(table_hbm, table_ref, load_sem.at[3])

    weights_load.start()
    for c in range(2):
        psi_load(c).start()
        for a in range(rows):
            plane_load(c, a).start()
    table_load.start()

    barrier = pltpu.get_barrier_semaphore()
    for tt in range(tn):

        @pl.when(t != tt)
        def column():
            pl.semaphore_signal(barrier, inc=1, device_id=(tt, p), device_id_type=MESH)

    for d in range(1, pn):
        pl.semaphore_signal(
            barrier, inc=1, device_id=(t, lax.rem(p + d, pn)), device_id_type=MESH
        )

    def pair_copy(q, r):
        return pltpu.make_async_remote_copy(
            src_ref=part.at[q * slab + r], dst_ref=pair_buf.at[q // 2, r],
            send_sem=pair_send.at[q // 2, r], recv_sem=pair_recv.at[q // 2, r],
            device_id=(t, partner), device_id_type=MESH,
        )

    def rs_copy(c, slot, r):
        q = 2 * c + core
        return pltpu.make_async_remote_copy(
            src_ref=part.at[q * slab + r], dst_ref=rs_buf.at[slot, r],
            send_sem=rs_send.at[c, r], recv_sem=rs_recv.at[slot, r],
            device_id=(t, q), device_id_type=MESH,
        )

    def t_copy(d, source, target):
        return pltpu.make_async_remote_copy(
            src_ref=planes.at[pl.ds(p * slab, slab)], dst_ref=t_buf.at[source],
            send_sem=t_send.at[d], recv_sem=t_recv.at[d],
            device_id=(target, p), device_id_type=MESH,
        )

    def t_sends(act):
        for d in range(1, tn):
            target = t + d if d % 2 else t - d

            @pl.when((target >= 0) & (target < tn))
            def send():
                act(t_copy(d, t, target))

    def t_arrivals():
        for d in range(1, tn):
            source = t - d if d % 2 else t + d

            @pl.when((source >= 0) & (source < tn))
            def arrived():
                t_copy(d, source, t).wait_recv()

    def a_copy(s, target, r):
        return pltpu.make_async_remote_copy(
            src_ref=a_buf.at[s, r], dst_ref=a_buf.at[s, r],
            send_sem=a_send.at[s, target, r], recv_sem=a_recv.at[s, r],
            device_id=(target, p), device_id_type=MESH,
        )

    def a_route(r, act, straight):
        for s in range(tn - 1):
            for target in range(s + 1, tn):
                if s % 2 == 0 or target == s + 1:

                    @pl.when(t == s)
                    def direct():
                        act(a_copy(s, target, r))

                elif straight:

                    @pl.when((t == s) & (core >= 0))
                    def far():
                        act(a_copy(s, target, r))

    def a_onward(r, act, wait, straight):
        for s in range(1, tn - 2, 2):

            @pl.when((t == s + 1) & ((core < 0) if straight else True))
            def onward():
                if wait:
                    a_copy(s, s + 1, r).wait_recv()
                for target in range(s + 2, tn):
                    act(a_copy(s, target, r))

    def a_arrivals(r):
        straight = r >= slab - HELD
        for s in range(tn - 1):
            here = t > s
            if s % 2 == 1 and s + 2 < tn:
                here = (t > s + 1) | ((t == s + 1) & (core >= 0)) if straight else t > s + 1

            @pl.when(here)
            def arrived():
                a_copy(s, s + 1, r).wait_recv()

    def start(copy):
        copy.start()

    def sent(copy):
        copy.wait_send()

    def g_up(source, target):
        return pltpu.make_async_remote_copy(
            src_ref=g_col.at[source], dst_ref=g_col.at[source],
            send_sem=g_send.at[target], recv_sem=g_recv.at[source],
            device_id=(target, p), device_id_type=MESH,
        )

    def g_share(d):
        return pltpu.make_async_remote_copy(
            src_ref=g_col, dst_ref=g_buf.at[p],
            send_sem=share_send, recv_sem=share_recv,
            device_id=(t, lax.rem(p + d, pn)), device_id_type=MESH,
        )

    def g_shares():
        every = g_buf.at[pl.ds(0, pn - 1)]
        return pltpu.make_async_remote_copy(
            src_ref=every, dst_ref=every, send_sem=share_send, recv_sem=share_recv,
            device_id=(t, partner), device_id_type=MESH,
        )

    group_of = lax.broadcasted_iota(jnp.int32, (rows, lanes), 1) // length
    per_block = groups // occupied_ref.shape[0]
    lane_group = lax.broadcasted_iota(jnp.int32, (length, lanes), 1) // length
    occ = 0.25 + 0.75 * occupied_ref[0].astype(jnp.float32) * jnp.ones((length, lanes), jnp.float32)
    for i in range(1, occupied_ref.shape[0]):
        level = 0.25 + 0.75 * occupied_ref[i].astype(jnp.float32)
        occ = jnp.where(lane_group >= i * per_block, level, occ)

    at_group = [group_of == g for g in range(groups)]
    def pick(options):
        chosen = options[0]
        for g in range(1, groups):
            chosen = jnp.where(at_group[g], options[g], chosen)
        return chosen

    def turn(value, steps):
        steps = steps % groups
        return value if steps == 0 else pltpu.roll(value, steps * length, 1)

    plane_rows = length * rows

    weights_load.wait()
    psi_load(0).wait()
    for a in range(rows):
        plane_load(0, a).wait()

    @pl.loop(0, length // FORWARD)
    def forward(i):
        @pl.when(i == early // FORWARD)
        def rest():
            psi_load(1).wait()
            for a in range(rows):
                plane_load(1, a).wait()

        density = []
        for j in range(FORWARD):
            x = i * FORWARD + j
            for q in range(length // groups):
                v = planes[x, :, q * lanes : (q + 1) * lanes]
                turned = [turn(v, s) for s in range(groups)]
                for g in range(groups):
                    y = q * groups + g
                    spread = pick([turned[(h - g) % groups] for h in range(groups)])
                    density.append(spread * psi_ref[x, y : y + 1, :])
        waves = split_product(jnp.concatenate(density, axis=0), weights_ref[...])
        for j in range(FORWARD):
            wave = waves[j * plane_rows : (j + 1) * plane_rows]
            modes = flat_dft([wave[y * rows : (y + 1) * rows] for y in range(length)])
            for m in range(length):
                spec[i * FORWARD + j, m] = modes[m]

    t_buf[t] = planes[pl.ds(p * slab, slab)]
    for x in range(length):
        psi_ref[x] = psi_ref[x] * occ
    for s in range(1, tn):

        @pl.when(s > t)
        def clear():
            a_buf[s] = jnp.zeros(a_buf.shape[1:], jnp.float32)
            g_col[s] = jnp.zeros(g_col.shape[1:], jnp.float32)

    gram_ref[...] = jnp.zeros_like(gram_ref)
    table_load.wait()
    pl.semaphore_wait(barrier, tn + pn - 2)
    t_sends(start)

    @pl.loop(0, length // MIDDLE)
    def middle(step):
        half = length // 2
        for j in range(MIDDLE):
            m = step * MIDDLE + j
            modes = flat_dft([spec[x, m] for x in range(length)])
            scaled = []
            for i in range(length):
                k = i if i <= half else i - half
                scaled.append(modes[i] * table_ref[m, k : k + 1, :])
            values = flat_dft_transposed(scaled)
            for x in range(length):
                spec[x, m] = values[x]

    per = chips // BACKWARD

    @pl.loop(0, 2 * slab * per)
    def backward(n):
        i = n // per
        first = lax.rem(n, per) * BACKWARD
        odd = lax.rem(i, 2)
        last = i == 2 * slab - 1
        away = (i == 0) | ((odd == 1) & jnp.logical_not(last))
        r = jnp.where(away, (i + 1) // 2, jnp.where(last, slab - 1, i // 2 - 1))
        side = jnp.where(away, 1 - core, core)
        owners = [2 * lax.rem(chip + 1 + first + j, chips) + side for j in range(BACKWARD)]
        values = []
        for q in owners:
            values += flat_dft_transposed([spec[q * slab + r, m] for m in range(length)])
        potentials = split_product(jnp.concatenate(values, axis=0), weights_ref[...])
        for j, owner in enumerate(owners):
            x = owner * slab + r
            potential = potentials[j * plane_rows : (j + 1) * plane_rows]
            for q in range(length // groups):
                terms = []
                for g in range(groups):
                    y = q * groups + g
                    terms.append(potential[y * rows : (y + 1) * rows] * psi_ref[x, y : y + 1, :])
                total = None
                for s in range(groups):
                    moved = turn(pick([terms[(h - s) % groups] for h in range(groups)]), -s)
                    total = moved if total is None else total + moved
                part[x, :, q * lanes : (q + 1) * lanes] = total

        @pl.when(away)
        def to_partner():
            for owner in owners:
                pair_copy(owner, r).start()

        @pl.when(jnp.logical_not(away))
        def to_owners():
            for j, owner in enumerate(owners):
                pair_copy(owner, r).wait_recv()

                @pl.when(first + j < chips - 1)
                def send():
                    x = owner * slab + r
                    part[x] = part[x] + pair_buf[owner // 2, r]
                    rs_copy(owner // 2, chip, r).start()

    def add_gram(r):
        every = jnp.concatenate([t_buf[s, r] for s in range(tn)], axis=0)
        gram_ref[...] += lax.dot_general(
            a_buf[t, r], every, (((1,), (1,)), ((), ())),
            precision=HIGHEST, preferred_element_type=jnp.float32,
        )

    @pl.loop(0, slab)
    def reduce(r):
        own = part[p * slab + r] + pair_buf[chip, r]
        for d in range(1, chips):
            c = lax.rem(chip + d, chips)
            rs_copy(c, c, r).wait_recv()
            own = own + rs_buf[c, r]
        a_buf[t, r] = own

        @pl.when(r < slab - HELD)
        def at_once():
            a_route(r, start, False)

        @pl.when(r == 1)
        def met():
            t_arrivals()

        @pl.when(r > 0)
        def earlier():
            add_gram(r - 1)

    add_gram(slab - 1)
    gram = gram_ref[...] * (1.0 / all_cells)
    fold = 128 // total_rows
    short = rows // fold
    g_col[t] = jnp.concatenate([gram[i * short : (i + 1) * short] for i in range(fold)], axis=1)
    for target in reversed(range(1, tn)):

        @pl.when(t < target)
        def upward():
            g_up(t, target).start()

    for r in range(slab - HELD):
        a_onward(r, start, True, False)
    for r in range(slab - HELD, slab):
        a_route(r, start, True)
    for s in range(tn - 1):

        @pl.when(t > s)
        def below():
            g_up(s, t).wait_recv()

    for d in range(1, pn):
        g_share(d).start()
    g_buf[p] = g_col[...]
    t_sends(sent)

    @pl.loop(0, slab)
    def drain(r):
        for c in range(chips):
            pair_copy(2 * c + 1 - core, r).wait_send()
        for d in range(1, chips):
            rs_copy(lax.rem(chip + d, chips), chip, r).wait_send()

    for r in range(slab - HELD, slab):
        a_onward(r, start, True, True)
    g_shares().wait_recv()
    blocks = []
    summed = g_buf[0]
    for q in range(1, pn):
        summed = summed + g_buf[q]
    for s in range(tn):
        blocks += [summed[s, :, i * total_rows : (i + 1) * total_rows] for i in range(fold)]
    square = jnp.concatenate(blocks, axis=0)
    square = jnp.concatenate(
        [square, jnp.zeros((total_rows, width - total_rows), jnp.float32)], axis=1
    )
    row_of = lax.broadcasted_iota(jnp.int32, (total_rows, width), 0)
    lane_of = lax.broadcasted_iota(jnp.int32, (total_rows, width), 1)
    row_block, lane_block = row_of // rows, lane_of // rows
    apart = lane_block - row_block
    odd = lax.rem(jnp.abs(apart), 2) == 1
    held = (apart == 0) | ((apart < 0) & odd) | ((apart > 0) & jnp.logical_not(odd))
    held = held & (row_block <= t) & (lane_block <= t)
    square = jnp.where(held, square, 0.0)
    padded = jnp.concatenate([square, jnp.zeros((width - total_rows, width), jnp.float32)], axis=0)
    both = square + jnp.transpose(padded)[:total_rows]
    symmetric = jnp.where(apart == 0, 0.5 * both, both)
    unit = (lane_of == row_of + total_rows) | ((lane_of == row_of) & (row_block > t))
    work = jnp.where(unit, 1.0, symmetric)
    line_of = lax.broadcasted_iota(jnp.int32, (PIVOTS, width), 0)
    strips = [work[k : k + PIVOTS, :] for k in range(0, total_rows, PIVOTS)]
    for k, strip in enumerate(strips):
        lines = [jnp.broadcast_to(strip[i : i + 1, :], strip.shape) for i in range(PIVOTS)]
        lane = [k * PIVOTS + i for i in range(PIVOTS)]
        corner = [
            [jnp.broadcast_to(line[:, h : h + 1], line.shape) for h in lane] for line in lines
        ]
        below = range(k + 1, len(strips))
        columns = [
            [jnp.broadcast_to(strips[g][:, h : h + 1], strip.shape) for g in below] for h in lane
        ]
        done = strip
        for i in range(PIVOTS):
            pivot = corner[i][i]
            inverse = 1.0 / pivot
            scaled = lines[i] * inverse
            done = jnp.where(line_of == i, lines[i] * (1.0 / jnp.sqrt(pivot)), done)
            for m in range(i + 1, PIVOTS):
                factor = corner[i][m] * inverse
                lines[m] = lines[m] - corner[i][m] * scaled
                for h in range(m, PIVOTS):
                    corner[m][h] = corner[m][h] - factor * corner[i][h]
                columns[m] = [c - d * factor for c, d in zip(columns[m], columns[i])]
            for g, column in zip(below, columns[i]):
                strips[g] = strips[g] - column * scaled
        strips[k] = done
    work = jnp.concatenate(strips, axis=0)
    keeping = (row_of < retained_ref[0]).astype(jnp.float32)
    inv_ref[...] = work * keeping
    mine = inv_ref[pl.ds(pl.multiple_of(t * rows, rows), rows), :][:, total_rows : 2 * total_rows]
    for x in range(slab):
        a_arrivals(x)
        every = jnp.concatenate([a_buf[s, x] for s in range(tn)], axis=0)
        out_ref[:, x, :] = jnp.dot(
            mine, every, precision=HIGHEST, preferred_element_type=jnp.float32
        )

    for target in range(1, tn):

        @pl.when(t < target)
        def ended():
            g_up(t, target).wait_send()

    g_shares().wait_send()
    for r in range(slab):
        a_route(r, sent, r >= slab - HELD)
        a_onward(r, sent, False, r >= slab - HELD)


def constants(length, groups):
    i = np.arange(length)
    phase = 2.0 * np.pi / length * (i[:, None] * i[None, :] % length)
    cas = np.kron(np.eye(groups), np.cos(phase) + np.sin(phase)).astype(np.float32)
    high = cas.astype(jnp.bfloat16)
    low = (cas - high.astype(np.float32)).astype(jnp.bfloat16)
    weights = np.concatenate([np.concatenate([high, low], 1)] * 2, 0)
    signed = np.where(i < length // 2, i, i - length)
    half = length // 2
    k = np.arange(half + 1)
    wave = (2.0 * np.pi / length) ** 2
    total = wave * ((k**2)[:, None, None] + (k**2)[None, :, None] + (signed**2)[None, None, :])
    coulomb = np.where(total > 0, 4 * np.pi / np.where(total > 0, total, 1.0), 0.0)
    fold = np.where((k == 0) | (k == half), 1.0, 2.0)
    coulomb = coulomb * fold[:, None, None] * fold[None, :, None] / length**3
    order = np.concatenate([np.arange(half + 1), np.arange(1, half)])
    table = np.tile(coulomb[order], (1, 1, groups)).astype(np.float32)
    return weights, table


def shards(tn, pn, targets, partners, occupied, retained):
    rows, length, cells = targets.shape
    lanes = partners.shape[2]
    groups = lanes // length
    slab = length // pn
    weights, table = constants(length, groups)
    total_rows = tn * rows
    width = -(-2 * total_rows // 128) * 128
    vmem = pl.BlockSpec(memory_space=pltpu.VMEM)
    smem = pl.BlockSpec(memory_space=pltpu.SMEM)
    hbm = pl.BlockSpec(memory_space=pl.ANY)
    planes = pltpu.VMEM((length, rows, cells), jnp.float32)
    block = pltpu.VMEM((tn, slab, rows, cells), jnp.float32)
    received = pltpu.VMEM((pn // 2, slab, rows, cells), jnp.float32)
    return pl.pallas_call(
        functools.partial(kernel, tn, pn),
        out_shape=pltpu.VMEM((rows, slab, cells), jnp.float32),
        in_specs=[hbm, hbm, hbm, hbm, smem, smem],
        out_specs=vmem,
        scratch_shapes=[
            planes,
            pltpu.VMEM(partners.shape, jnp.float32),
            pltpu.VMEM(weights.shape, weights.dtype),
            pltpu.VMEM(table.shape, jnp.float32),
            pltpu.VMEM((length, length + 1, rows, lanes), jnp.float32),
            planes,
            received,
            received,
            block,
            block,
            pltpu.VMEM((rows, total_rows), jnp.float32),
            pltpu.VMEM((tn, rows * total_rows // 128, 128), jnp.float32),
            pltpu.VMEM((pn, tn, rows * total_rows // 128, 128), jnp.float32),
            pltpu.VMEM((total_rows, width), jnp.float32),
        ],
        compiler_params=pltpu.CompilerParams(collective_id=0, has_side_effects=True),
        name="exchange",
    )(targets, partners, jnp.asarray(weights), jnp.asarray(table), occupied, retained)


def solution(mesh):
    return jax.shard_map(
        functools.partial(shards, mesh.shape["tgt"], mesh.shape["ptr"]),
        mesh=mesh,
        in_specs=(P("tgt", None, None), P(None, None, "ptr"), P("ptr"), P()),
        out_specs=P("tgt", "ptr", None),
        check_vma=False,
    )
```

```python
import functools
import math

import jax
import jax.numpy as jnp
import numpy as np
from jax import lax
from jax.experimental import pallas as pl
from jax.experimental.pallas import tpu as pltpu
from jax.sharding import PartitionSpec as P

HIGHEST = lax.Precision.HIGHEST
MESH = pl.DeviceIdType.MESH
FORWARD = 8
BACKWARD = 4
PIVOTS = 8
MIDDLE = 2
HELD = 2


def turned_by(n, k, re, im):
    c, s = math.cos(2 * math.pi * k / n), math.sin(2 * math.pi * k / n)
    return c * re + s * im, c * im - s * re


def real_dft(values):
    n = len(values)
    if n == 1:
        return [values[0]], [None]
    if n == 2:
        return [values[0] + values[1], values[0] - values[1]], [None, None]
    half, quarter, eighth = n // 2, n // 4, n // 8
    even_re, even_im = real_dft(values[0::2])
    one_re, one_im = real_dft(values[1::4])
    three_re, three_im = real_dft(values[3::4])
    re, im = [None] * (half + 1), [None] * (half + 1)
    total = one_re[0] + three_re[0]
    re[0], re[half] = even_re[0] + total, even_re[0] - total
    re[quarter], im[quarter] = even_re[quarter], three_re[0] - one_re[0]
    for k in range(1, eighth + 1):
        if 2 * k == quarter:
            c = math.sqrt(0.5)
            a, b = c * (one_re[k] - three_re[k]), c * (one_re[k] + three_re[k])
            re[k], re[half - k] = even_re[k] + a, even_re[k] - a
            im[k], im[half - k] = even_im[k] - b, -b - even_im[k]
            continue
        one = turned_by(n, k, one_re[k], one_im[k])
        three = turned_by(n, 3 * k, three_re[k], three_im[k])
        sum_re, sum_im = one[0] + three[0], one[1] + three[1]
        gap_re, gap_im = one[0] - three[0], one[1] - three[1]
        re[k], re[half - k] = even_re[k] + sum_re, even_re[k] - sum_re
        im[k], im[half - k] = even_im[k] + sum_im, sum_im - even_im[k]
        mirror = quarter - k
        re[quarter + k], re[mirror] = even_re[mirror] + gap_im, even_re[mirror] - gap_im
        im[quarter + k], im[mirror] = -gap_re - even_im[mirror], even_im[mirror] - gap_re
    return re, im


def real_dft_transposed(re, im):
    half = len(re) - 1
    if half == 0:
        return [re[0]]
    if half == 1:
        return [re[0] + re[1], re[0] - re[1]]
    n = 2 * half
    quarter, eighth = half // 2, half // 4
    even_re, even_im = [None] * (quarter + 1), [None] * (quarter + 1)
    one_re, one_im = [None] * (eighth + 1), [None] * (eighth + 1)
    three_re, three_im = [None] * (eighth + 1), [None] * (eighth + 1)
    even_re[0], total = re[0] + re[half], re[0] - re[half]
    even_re[quarter] = re[quarter]
    one_re[0], three_re[0] = total - im[quarter], total + im[quarter]
    for k in range(1, eighth + 1):
        sum_re, even_re[k] = re[k] - re[half - k], re[k] + re[half - k]
        sum_im, even_im[k] = im[k] + im[half - k], im[k] - im[half - k]
        if 2 * k == quarter:
            c = math.sqrt(0.5)
            one_re[k], three_re[k] = c * (sum_re - sum_im), -c * (sum_re + sum_im)
            continue
        mirror = quarter - k
        even_re[mirror], gap_im = re[quarter + k] + re[mirror], re[quarter + k] - re[mirror]
        even_im[mirror] = im[mirror] - im[quarter + k]
        gap_re = -(im[quarter + k] + im[mirror])
        one = sum_re + gap_re, sum_im + gap_im
        three = sum_re - gap_re, sum_im - gap_im
        one_re[k], one_im[k] = turned_by(n, -k, *one)
        three_re[k], three_im[k] = turned_by(n, -3 * k, *three)
    values = [None] * n
    values[0::2] = real_dft_transposed(even_re, even_im)
    values[1::4] = real_dft_transposed(one_re, one_im)
    values[3::4] = real_dft_transposed(three_re, three_im)
    return values


def flat_dft(values):
    re, im = real_dft(values)
    return re + im[1:-1]


def flat_dft_transposed(modes):
    half = len(modes) // 2
    return real_dft_transposed(modes[: half + 1], [None] + modes[half + 1 :] + [None])


def split_product(field, weights):
    width = field.shape[1]
    high = field.astype(jnp.bfloat16)
    low = (field - high.astype(jnp.float32)).astype(jnp.bfloat16)
    both = jnp.dot(
        jnp.concatenate([high, low], axis=1), weights, preferred_element_type=jnp.float32
    )
    return both[:, :width] + both[:, width:]


def kernel(
    tn, pn, t_hbm, psi_hbm, weights_hbm, table_hbm, occupied_ref, retained_ref, out_ref,
    planes, psi_ref, weights_ref, table_ref, spec, part, pair_buf, rs_buf, t_buf, a_buf,
    gram_ref, g_col, g_buf, inv_ref,
):
    slab = planes.shape[0] // pn
    rows = planes.shape[1]
    dma = pltpu.SemaphoreType.DMA
    pl.run_scoped(
        functools.partial(
            exchange, tn, pn, t_hbm, psi_hbm, weights_hbm, table_hbm, occupied_ref, retained_ref,
            out_ref, planes, psi_ref, weights_ref, table_ref, spec, part, pair_buf, rs_buf, t_buf,
            a_buf, gram_ref, g_col, g_buf, inv_ref,
        ),
        dma((2, rows)), dma((4,)), dma((pn // 2, slab)), dma((pn // 2, slab)),
        dma((pn // 2, slab)), dma((pn // 2, slab)), dma((tn,)), dma((tn,)),
        dma((tn, tn, slab)), dma((tn, slab)), dma((tn,)), dma((tn,)), dma, dma,
    )


def exchange(
    tn, pn, t_hbm, psi_hbm, weights_hbm, table_hbm, occupied_ref, retained_ref, out_ref,
    planes, psi_ref, weights_ref, table_ref, spec, part, pair_buf, rs_buf, t_buf, a_buf,
    gram_ref, g_col, g_buf, inv_ref,
    plane_sem, load_sem, pair_send, pair_recv, rs_send, rs_recv, t_send, t_recv,
    a_send, a_recv, g_send, g_recv, share_send, share_recv,
):
    t, p = lax.axis_index("tgt"), lax.axis_index("ptr")
    length, rows, cells = planes.shape
    lanes = psi_ref.shape[2]
    groups = lanes // length
    slab = length // pn
    all_cells = length * cells
    total_rows = tn * rows
    width = inv_ref.shape[1]
    chips = pn // 2
    chip, core = p // 2, lax.rem(p, 2)
    partner = p + 1 - 2 * core
    early = length // 4

    def plane_load(c, a):
        xs = pl.ds(0, early) if c == 0 else pl.ds(early, length - early)
        return pltpu.make_async_copy(t_hbm.at[a, xs, :], planes.at[xs, a, :], plane_sem.at[c, a])

    def psi_load(c):
        xs = pl.ds(0, early) if c == 0 else pl.ds(early, length - early)
        return pltpu.make_async_copy(psi_hbm.at[xs], psi_ref.at[xs], load_sem.at[c])

    weights_load = pltpu.make_async_copy(weights_hbm, weights_ref, load_sem.at[2])
    table_load = pltpu.make_async_copy(table_hbm, table_ref, load_sem.at[3])

    weights_load.start()
    for c in range(2):
        psi_load(c).start()
        for a in range(rows):
            plane_load(c, a).start()
    table_load.start()

    barrier = pltpu.get_barrier_semaphore()
    for tt in range(tn):

        @pl.when(t != tt)
        def column():
            pl.semaphore_signal(barrier, inc=1, device_id=(tt, p), device_id_type=MESH)

    for d in range(1, pn):
        pl.semaphore_signal(
            barrier, inc=1, device_id=(t, lax.rem(p + d, pn)), device_id_type=MESH
        )

    def pair_copy(q, r):
        return pltpu.make_async_remote_copy(
            src_ref=part.at[q * slab + r], dst_ref=pair_buf.at[q // 2, r],
            send_sem=pair_send.at[q // 2, r], recv_sem=pair_recv.at[q // 2, r],
            device_id=(t, partner), device_id_type=MESH,
        )

    def rs_copy(c, slot, r):
        q = 2 * c + core
        return pltpu.make_async_remote_copy(
            src_ref=part.at[q * slab + r], dst_ref=rs_buf.at[slot, r],
            send_sem=rs_send.at[c, r], recv_sem=rs_recv.at[slot, r],
            device_id=(t, q), device_id_type=MESH,
        )

    def t_copy(d, source, target):
        return pltpu.make_async_remote_copy(
            src_ref=planes.at[pl.ds(p * slab, slab)], dst_ref=t_buf.at[source],
            send_sem=t_send.at[d], recv_sem=t_recv.at[d],
            device_id=(target, p), device_id_type=MESH,
        )

    def t_sends(act):
        for d in range(1, tn):
            target = t + d if d % 2 else t - d

            @pl.when((target >= 0) & (target < tn))
            def send():
                act(t_copy(d, t, target))

    def t_arrivals():
        for d in range(1, tn):
            source = t - d if d % 2 else t + d

            @pl.when((source >= 0) & (source < tn))
            def arrived():
                t_copy(d, source, t).wait_recv()

    def a_copy(s, target, r):
        return pltpu.make_async_remote_copy(
            src_ref=a_buf.at[s, r], dst_ref=a_buf.at[s, r],
            send_sem=a_send.at[s, target, r], recv_sem=a_recv.at[s, r],
            device_id=(target, p), device_id_type=MESH,
        )

    def a_route(r, act, straight):
        for s in range(tn - 1):
            for target in range(s + 1, tn):
                if s % 2 == 0 or target == s + 1:

                    @pl.when(t == s)
                    def direct():
                        act(a_copy(s, target, r))

                elif straight:

                    @pl.when((t == s) & (core >= 0))
                    def far():
                        act(a_copy(s, target, r))

    def a_onward(r, act, wait, straight):
        for s in range(1, tn - 2, 2):

            @pl.when((t == s + 1) & ((core < 0) if straight else True))
            def onward():
                if wait:
                    a_copy(s, s + 1, r).wait_recv()
                for target in range(s + 2, tn):
                    act(a_copy(s, target, r))

    def a_arrivals(r):
        straight = r >= slab - HELD
        for s in range(tn - 1):
            here = t > s
            if s % 2 == 1 and s + 2 < tn:
                here = (t > s + 1) | ((t == s + 1) & (core >= 0)) if straight else t > s + 1

            @pl.when(here)
            def arrived():
                a_copy(s, s + 1, r).wait_recv()

    def start(copy):
        copy.start()

    def sent(copy):
        copy.wait_send()

    def g_up(source, target):
        return pltpu.make_async_remote_copy(
            src_ref=g_col.at[source], dst_ref=g_col.at[source],
            send_sem=g_send.at[target], recv_sem=g_recv.at[source],
            device_id=(target, p), device_id_type=MESH,
        )

    def g_share(d):
        return pltpu.make_async_remote_copy(
            src_ref=g_col, dst_ref=g_buf.at[p],
            send_sem=share_send, recv_sem=share_recv,
            device_id=(t, lax.rem(p + d, pn)), device_id_type=MESH,
        )

    def g_shares():
        every = g_buf.at[pl.ds(0, pn - 1)]
        return pltpu.make_async_remote_copy(
            src_ref=every, dst_ref=every, send_sem=share_send, recv_sem=share_recv,
            device_id=(t, partner), device_id_type=MESH,
        )

    group_of = lax.broadcasted_iota(jnp.int32, (rows, lanes), 1) // length
    per_block = groups // occupied_ref.shape[0]
    lane_group = lax.broadcasted_iota(jnp.int32, (length, lanes), 1) // length
    occ = 0.25 + 0.75 * occupied_ref[0].astype(jnp.float32) * jnp.ones((length, lanes), jnp.float32)
    for i in range(1, occupied_ref.shape[0]):
        level = 0.25 + 0.75 * occupied_ref[i].astype(jnp.float32)
        occ = jnp.where(lane_group >= i * per_block, level, occ)

    at_group = [group_of == g for g in range(groups)]
    def pick(options):
        chosen = options[0]
        for g in range(1, groups):
            chosen = jnp.where(at_group[g], options[g], chosen)
        return chosen

    def turn(value, steps):
        steps = steps % groups
        return value if steps == 0 else pltpu.roll(value, steps * length, 1)

    plane_rows = length * rows

    weights_load.wait()
    psi_load(0).wait()
    for a in range(rows):
        plane_load(0, a).wait()

    @pl.loop(0, length // FORWARD)
    def forward(i):
        @pl.when(i == early // FORWARD)
        def rest():
            psi_load(1).wait()
            for a in range(rows):
                plane_load(1, a).wait()

        density = []
        for j in range(FORWARD):
            x = i * FORWARD + j
            for q in range(length // groups):
                v = planes[x, :, q * lanes : (q + 1) * lanes]
                turned = [turn(v, s) for s in range(groups)]
                for g in range(groups):
                    y = q * groups + g
                    spread = pick([turned[(h - g) % groups] for h in range(groups)])
                    density.append(spread * psi_ref[x, y : y + 1, :])
        waves = split_product(jnp.concatenate(density, axis=0), weights_ref[...])
        for j in range(FORWARD):
            wave = waves[j * plane_rows : (j + 1) * plane_rows]
            modes = flat_dft([wave[y * rows : (y + 1) * rows] for y in range(length)])
            for m in range(length):
                spec[i * FORWARD + j, m] = modes[m]

    for x in range(length):
        psi_ref[x] = psi_ref[x] * occ
    table_load.wait()
    pl.semaphore_wait(barrier, tn + pn - 2)
    t_sends(start)

    @pl.loop(0, length // MIDDLE)
    def middle(step):
        half = length // 2
        for j in range(MIDDLE):
            m = step * MIDDLE + j
            modes = flat_dft([spec[x, m] for x in range(length)])
            scaled = []
            for i in range(length):
                k = i if i <= half else i - half
                scaled.append(modes[i] * table_ref[m, k : k + 1, :])
            values = flat_dft_transposed(scaled)
            for x in range(length):
                spec[x, m] = values[x]

    per = chips // BACKWARD

    @pl.loop(0, 2 * slab * per)
    def backward(n):
        i = n // per
        first = lax.rem(n, per) * BACKWARD
        odd = lax.rem(i, 2)
        last = i == 2 * slab - 1
        away = (i == 0) | ((odd == 1) & jnp.logical_not(last))
        r = jnp.where(away, (i + 1) // 2, jnp.where(last, slab - 1, i // 2 - 1))
        side = jnp.where(away, 1 - core, core)
        if chips == BACKWARD == 4:
            order = [chips - 1 - chip, lax.rem(chip + 2, chips), chip + 1 - 2 * lax.rem(chip, 2), chip]
        else:
            order = [lax.rem(chip + 1 + first + j, chips) for j in range(BACKWARD)]
        owners = [2 * c + side for c in order]
        values = []
        for q in owners:
            values += flat_dft_transposed([spec[q * slab + r, m] for m in range(length)])
        potentials = split_product(jnp.concatenate(values, axis=0), weights_ref[...])
        for j, owner in enumerate(owners):
            x = owner * slab + r
            potential = potentials[j * plane_rows : (j + 1) * plane_rows]
            for q in range(length // groups):
                terms = []
                for g in range(groups):
                    y = q * groups + g
                    terms.append(potential[y * rows : (y + 1) * rows] * psi_ref[x, y : y + 1, :])
                total = None
                for s in range(groups):
                    moved = turn(pick([terms[(h - s) % groups] for h in range(groups)]), -s)
                    total = moved if total is None else total + moved
                part[x, :, q * lanes : (q + 1) * lanes] = total

        @pl.when(away)
        def to_partner():
            for owner in owners:
                pair_copy(owner, r).start()

        @pl.when(jnp.logical_not(away))
        def to_owners():
            for j, owner in enumerate(owners):
                pair_copy(owner, r).wait_recv()

                @pl.when(first + j < chips - 1)
                def send():
                    x = owner * slab + r
                    part[x] = part[x] + pair_buf[owner // 2, r]
                    rs_copy(owner // 2, chip, r).start()

    t_buf[t] = planes[pl.ds(p * slab, slab)]
    for s in range(1, tn):

        @pl.when(s > t)
        def clear():
            a_buf[s] = jnp.zeros(a_buf.shape[1:], jnp.float32)
            g_col[s] = jnp.zeros(g_col.shape[1:], jnp.float32)

    gram_ref[...] = jnp.zeros_like(gram_ref)
    def add_gram(r):
        every = jnp.concatenate([t_buf[s, r] for s in range(tn)], axis=0)
        gram_ref[...] += lax.dot_general(
            a_buf[t, r], every, (((1,), (1,)), ((), ())),
            precision=HIGHEST, preferred_element_type=jnp.float32,
        )

    @pl.loop(0, slab)
    def reduce(r):
        own = part[p * slab + r] + pair_buf[chip, r]
        for d in range(1, chips):
            c = lax.rem(chip + d, chips)
            rs_copy(c, c, r).wait_recv()
            own = own + rs_buf[c, r]
        a_buf[t, r] = own

        @pl.when(r < slab - HELD)
        def at_once():
            a_route(r, start, False)

        @pl.when(r == 1)
        def met():
            t_arrivals()

        @pl.when(r > 0)
        def earlier():
            add_gram(r - 1)

    add_gram(slab - 1)
    gram = gram_ref[...] * (1.0 / all_cells)
    fold = 128 // total_rows
    short = rows // fold
    g_col[t] = jnp.concatenate([gram[i * short : (i + 1) * short] for i in range(fold)], axis=1)
    for target in reversed(range(1, tn)):

        @pl.when(t < target)
        def upward():
            g_up(t, target).start()

    for r in range(slab - HELD):
        a_onward(r, start, True, False)
    for r in range(slab - HELD, slab):
        a_route(r, start, True)
    for s in range(tn - 1):

        @pl.when(t > s)
        def below():
            g_up(s, t).wait_recv()

    for d in range(1, pn):
        g_share(d).start()
    g_buf[p] = g_col[...]
    t_sends(sent)

    @pl.loop(0, slab)
    def drain(r):
        for c in range(chips):
            pair_copy(2 * c + 1 - core, r).wait_send()
        for d in range(1, chips):
            rs_copy(lax.rem(chip + d, chips), chip, r).wait_send()

    for r in range(slab - HELD, slab):
        a_onward(r, start, True, True)
    for target in range(1, tn):

        @pl.when(t < target)
        def ended():
            g_up(t, target).wait_send()

    for r in range(slab - HELD):
        a_route(r, sent, False)
        a_onward(r, sent, False, False)
    g_shares().wait_recv()
    blocks = []
    summed = g_buf[0]
    for q in range(1, pn):
        summed = summed + g_buf[q]
    for s in range(tn):
        blocks += [summed[s, :, i * total_rows : (i + 1) * total_rows] for i in range(fold)]
    square = jnp.concatenate(blocks, axis=0)
    square = jnp.concatenate(
        [square, jnp.zeros((total_rows, width - total_rows), jnp.float32)], axis=1
    )
    row_of = lax.broadcasted_iota(jnp.int32, (total_rows, width), 0)
    lane_of = lax.broadcasted_iota(jnp.int32, (total_rows, width), 1)
    row_block, lane_block = row_of // rows, lane_of // rows
    apart = lane_block - row_block
    odd = lax.rem(jnp.abs(apart), 2) == 1
    held = (apart == 0) | ((apart < 0) & odd) | ((apart > 0) & jnp.logical_not(odd))
    held = held & (row_block <= t) & (lane_block <= t)
    square = jnp.where(held, square, 0.0)
    padded = jnp.concatenate([square, jnp.zeros((width - total_rows, width), jnp.float32)], axis=0)
    both = square + jnp.transpose(padded)[:total_rows]
    symmetric = jnp.where(apart == 0, 0.5 * both, both)
    unit = (lane_of == row_of + total_rows) | ((lane_of == row_of) & (row_block > t))
    work = jnp.where(unit, 1.0, symmetric)
    line_of = lax.broadcasted_iota(jnp.int32, (PIVOTS, width), 0)
    strips = [work[k : k + PIVOTS, :] for k in range(0, total_rows, PIVOTS)]
    for k, strip in enumerate(strips):
        lines = [jnp.broadcast_to(strip[i : i + 1, :], strip.shape) for i in range(PIVOTS)]
        lane = [k * PIVOTS + i for i in range(PIVOTS)]
        corner = [
            [jnp.broadcast_to(line[:, h : h + 1], line.shape) for h in lane] for line in lines
        ]
        below = range(k + 1, len(strips))
        columns = [
            [jnp.broadcast_to(strips[g][:, h : h + 1], strip.shape) for g in below] for h in lane
        ]
        done = strip
        for i in range(PIVOTS):
            pivot = corner[i][i]
            inverse = 1.0 / pivot
            scaled = lines[i] * inverse
            done = jnp.where(line_of == i, lines[i] * (1.0 / jnp.sqrt(pivot)), done)
            for m in range(i + 1, PIVOTS):
                factor = corner[i][m] * inverse
                lines[m] = lines[m] - corner[i][m] * scaled
                for h in range(m, PIVOTS):
                    corner[m][h] = corner[m][h] - factor * corner[i][h]
                columns[m] = [c - d * factor for c, d in zip(columns[m], columns[i])]
            for g, column in zip(below, columns[i]):
                strips[g] = strips[g] - column * scaled
        strips[k] = done
    work = jnp.concatenate(strips, axis=0)
    keeping = (row_of < retained_ref[0]).astype(jnp.float32)
    inv_ref[...] = work * keeping
    mine = inv_ref[pl.ds(pl.multiple_of(t * rows, rows), rows), :][:, total_rows : 2 * total_rows]
    for x in range(slab):
        a_arrivals(x)
        every = jnp.concatenate([a_buf[s, x] for s in range(tn)], axis=0)
        out_ref[:, x, :] = jnp.dot(
            mine, every, precision=HIGHEST, preferred_element_type=jnp.float32
        )

    g_shares().wait_send()
    for r in range(slab - HELD, slab):
        a_route(r, sent, True)
        a_onward(r, sent, False, True)


def constants(length, groups):
    i = np.arange(length)
    phase = 2.0 * np.pi / length * (i[:, None] * i[None, :] % length)
    cas = np.kron(np.eye(groups), np.cos(phase) + np.sin(phase)).astype(np.float32)
    high = cas.astype(jnp.bfloat16)
    low = (cas - high.astype(np.float32)).astype(jnp.bfloat16)
    weights = np.concatenate([np.concatenate([high, low], 1)] * 2, 0)
    signed = np.where(i < length // 2, i, i - length)
    half = length // 2
    k = np.arange(half + 1)
    wave = (2.0 * np.pi / length) ** 2
    total = wave * ((k**2)[:, None, None] + (k**2)[None, :, None] + (signed**2)[None, None, :])
    coulomb = np.where(total > 0, 4 * np.pi / np.where(total > 0, total, 1.0), 0.0)
    fold = np.where((k == 0) | (k == half), 1.0, 2.0)
    coulomb = coulomb * fold[:, None, None] * fold[None, :, None] / length**3
    order = np.concatenate([np.arange(half + 1), np.arange(1, half)])
    table = np.tile(coulomb[order], (1, 1, groups)).astype(np.float32)
    return weights, table


def shards(tn, pn, targets, partners, occupied, retained):
    rows, length, cells = targets.shape
    lanes = partners.shape[2]
    groups = lanes // length
    slab = length // pn
    weights, table = constants(length, groups)
    total_rows = tn * rows
    width = -(-2 * total_rows // 128) * 128
    vmem = pl.BlockSpec(memory_space=pltpu.VMEM)
    smem = pl.BlockSpec(memory_space=pltpu.SMEM)
    hbm = pl.BlockSpec(memory_space=pl.ANY)
    planes = pltpu.VMEM((length, rows, cells), jnp.float32)
    block = pltpu.VMEM((tn, slab, rows, cells), jnp.float32)
    received = pltpu.VMEM((pn // 2, slab, rows, cells), jnp.float32)
    return pl.pallas_call(
        functools.partial(kernel, tn, pn),
        out_shape=pltpu.VMEM((rows, slab, cells), jnp.float32),
        in_specs=[hbm, hbm, hbm, hbm, smem, smem],
        out_specs=vmem,
        scratch_shapes=[
            planes,
            pltpu.VMEM(partners.shape, jnp.float32),
            pltpu.VMEM(weights.shape, weights.dtype),
            pltpu.VMEM(table.shape, jnp.float32),
            pltpu.VMEM((length, length + 1, rows, lanes), jnp.float32),
            planes,
            received,
            received,
            block,
            block,
            pltpu.VMEM((rows, total_rows), jnp.float32),
            pltpu.VMEM((tn, rows * total_rows // 128, 128), jnp.float32),
            pltpu.VMEM((pn, tn, rows * total_rows // 128, 128), jnp.float32),
            pltpu.VMEM((total_rows, width), jnp.float32),
        ],
        compiler_params=pltpu.CompilerParams(collective_id=0, has_side_effects=True),
        name="exchange",
    )(targets, partners, jnp.asarray(weights), jnp.asarray(table), occupied, retained)


def solution(mesh):
    return jax.shard_map(
        functools.partial(shards, mesh.shape["tgt"], mesh.shape["ptr"]),
        mesh=mesh,
        in_specs=(P("tgt", None, None), P(None, None, "ptr"), P("ptr"), P()),
        out_specs=P("tgt", "ptr", None),
        check_vma=False,
    )
```

```python
import functools
import math

import jax
import jax.numpy as jnp
import numpy as np
from jax import lax
from jax.experimental import pallas as pl
from jax.experimental.pallas import tpu as pltpu
from jax.sharding import PartitionSpec as P

HIGHEST = lax.Precision.HIGHEST
MESH = pl.DeviceIdType.MESH
FORWARD = 8
BACKWARD = 4
PIVOTS = 8
MIDDLE = 2
HELD = 2


def turned_by(n, k, re, im):
    c, s = math.cos(2 * math.pi * k / n), math.sin(2 * math.pi * k / n)
    return c * re + s * im, c * im - s * re


def real_dft(values):
    n = len(values)
    if n == 1:
        return [values[0]], [None]
    if n == 2:
        return [values[0] + values[1], values[0] - values[1]], [None, None]
    half, quarter, eighth = n // 2, n // 4, n // 8
    even_re, even_im = real_dft(values[0::2])
    one_re, one_im = real_dft(values[1::4])
    three_re, three_im = real_dft(values[3::4])
    re, im = [None] * (half + 1), [None] * (half + 1)
    total = one_re[0] + three_re[0]
    re[0], re[half] = even_re[0] + total, even_re[0] - total
    re[quarter], im[quarter] = even_re[quarter], three_re[0] - one_re[0]
    for k in range(1, eighth + 1):
        if 2 * k == quarter:
            c = math.sqrt(0.5)
            a, b = c * (one_re[k] - three_re[k]), c * (one_re[k] + three_re[k])
            re[k], re[half - k] = even_re[k] + a, even_re[k] - a
            im[k], im[half - k] = even_im[k] - b, -b - even_im[k]
            continue
        one = turned_by(n, k, one_re[k], one_im[k])
        three = turned_by(n, 3 * k, three_re[k], three_im[k])
        sum_re, sum_im = one[0] + three[0], one[1] + three[1]
        gap_re, gap_im = one[0] - three[0], one[1] - three[1]
        re[k], re[half - k] = even_re[k] + sum_re, even_re[k] - sum_re
        im[k], im[half - k] = even_im[k] + sum_im, sum_im - even_im[k]
        mirror = quarter - k
        re[quarter + k], re[mirror] = even_re[mirror] + gap_im, even_re[mirror] - gap_im
        im[quarter + k], im[mirror] = -gap_re - even_im[mirror], even_im[mirror] - gap_re
    return re, im


def real_dft_transposed(re, im):
    half = len(re) - 1
    if half == 0:
        return [re[0]]
    if half == 1:
        return [re[0] + re[1], re[0] - re[1]]
    n = 2 * half
    quarter, eighth = half // 2, half // 4
    even_re, even_im = [None] * (quarter + 1), [None] * (quarter + 1)
    one_re, one_im = [None] * (eighth + 1), [None] * (eighth + 1)
    three_re, three_im = [None] * (eighth + 1), [None] * (eighth + 1)
    even_re[0], total = re[0] + re[half], re[0] - re[half]
    even_re[quarter] = re[quarter]
    one_re[0], three_re[0] = total - im[quarter], total + im[quarter]
    for k in range(1, eighth + 1):
        sum_re, even_re[k] = re[k] - re[half - k], re[k] + re[half - k]
        sum_im, even_im[k] = im[k] + im[half - k], im[k] - im[half - k]
        if 2 * k == quarter:
            c = math.sqrt(0.5)
            one_re[k], three_re[k] = c * (sum_re - sum_im), -c * (sum_re + sum_im)
            continue
        mirror = quarter - k
        even_re[mirror], gap_im = re[quarter + k] + re[mirror], re[quarter + k] - re[mirror]
        even_im[mirror] = im[mirror] - im[quarter + k]
        gap_re = -(im[quarter + k] + im[mirror])
        one = sum_re + gap_re, sum_im + gap_im
        three = sum_re - gap_re, sum_im - gap_im
        one_re[k], one_im[k] = turned_by(n, -k, *one)
        three_re[k], three_im[k] = turned_by(n, -3 * k, *three)
    values = [None] * n
    values[0::2] = real_dft_transposed(even_re, even_im)
    values[1::4] = real_dft_transposed(one_re, one_im)
    values[3::4] = real_dft_transposed(three_re, three_im)
    return values


def flat_dft(values):
    re, im = real_dft(values)
    return re + im[1:-1]


def flat_dft_transposed(modes):
    half = len(modes) // 2
    return real_dft_transposed(modes[: half + 1], [None] + modes[half + 1 :] + [None])


def split_product(field, weights):
    width = field.shape[1]
    high = field.astype(jnp.bfloat16)
    low = (field - high.astype(jnp.float32)).astype(jnp.bfloat16)
    both = jnp.dot(
        jnp.concatenate([high, low], axis=1), weights, preferred_element_type=jnp.float32
    )
    return both[:, :width] + both[:, width:]


def kernel(
    tn, pn, t_hbm, psi_hbm, weights_hbm, table_hbm, occupied_ref, retained_ref, out_ref,
    planes, psi_ref, weights_ref, table_ref, spec, part, pair_buf, rs_buf, t_buf, a_buf,
    gram_ref, g_col, g_buf, inv_ref,
):
    slab = planes.shape[0] // pn
    rows = planes.shape[1]
    dma = pltpu.SemaphoreType.DMA
    pl.run_scoped(
        functools.partial(
            exchange, tn, pn, t_hbm, psi_hbm, weights_hbm, table_hbm, occupied_ref, retained_ref,
            out_ref, planes, psi_ref, weights_ref, table_ref, spec, part, pair_buf, rs_buf, t_buf,
            a_buf, gram_ref, g_col, g_buf, inv_ref,
        ),
        dma((2, rows)), dma((4,)), dma((pn // 2, slab)), dma((pn // 2, slab)),
        dma((pn // 2, slab)), dma((pn // 2, slab)), dma((tn,)), dma((tn,)),
        dma((tn, tn, slab)), dma((tn, slab)), dma((tn,)), dma((tn,)), dma, dma,
    )


def exchange(
    tn, pn, t_hbm, psi_hbm, weights_hbm, table_hbm, occupied_ref, retained_ref, out_ref,
    planes, psi_ref, weights_ref, table_ref, spec, part, pair_buf, rs_buf, t_buf, a_buf,
    gram_ref, g_col, g_buf, inv_ref,
    plane_sem, load_sem, pair_send, pair_recv, rs_send, rs_recv, t_send, t_recv,
    a_send, a_recv, g_send, g_recv, share_send, share_recv,
):
    t, p = lax.axis_index("tgt"), lax.axis_index("ptr")
    length, rows, cells = planes.shape
    lanes = psi_ref.shape[2]
    groups = lanes // length
    slab = length // pn
    all_cells = length * cells
    total_rows = tn * rows
    width = inv_ref.shape[1]
    chips = pn // 2
    chip, core = p // 2, lax.rem(p, 2)
    partner = p + 1 - 2 * core
    early = length // 4

    def plane_load(c, a):
        xs = pl.ds(0, early) if c == 0 else pl.ds(early, length - early)
        return pltpu.make_async_copy(t_hbm.at[a, xs, :], planes.at[xs, a, :], plane_sem.at[c, a])

    def psi_load(c):
        xs = pl.ds(0, early) if c == 0 else pl.ds(early, length - early)
        return pltpu.make_async_copy(psi_hbm.at[xs], psi_ref.at[xs], load_sem.at[c])

    weights_load = pltpu.make_async_copy(weights_hbm, weights_ref, load_sem.at[2])
    table_load = pltpu.make_async_copy(table_hbm, table_ref, load_sem.at[3])

    weights_load.start()
    for c in range(2):
        psi_load(c).start()
        for a in range(rows):
            plane_load(c, a).start()
    table_load.start()

    barrier = pltpu.get_barrier_semaphore()
    for tt in range(tn):

        @pl.when(t != tt)
        def column():
            pl.semaphore_signal(barrier, inc=1, device_id=(tt, p), device_id_type=MESH)

    for d in range(1, pn):
        pl.semaphore_signal(
            barrier, inc=1, device_id=(t, lax.rem(p + d, pn)), device_id_type=MESH
        )

    def pair_copy(q, r):
        return pltpu.make_async_remote_copy(
            src_ref=part.at[q * slab + r], dst_ref=pair_buf.at[q // 2, r],
            send_sem=pair_send.at[q // 2, r], recv_sem=pair_recv.at[q // 2, r],
            device_id=(t, partner), device_id_type=MESH,
        )

    def rs_copy(c, slot, r):
        q = 2 * c + core
        return pltpu.make_async_remote_copy(
            src_ref=part.at[q * slab + r], dst_ref=rs_buf.at[slot, r],
            send_sem=rs_send.at[c, r], recv_sem=rs_recv.at[slot, r],
            device_id=(t, q), device_id_type=MESH,
        )

    def t_copy(d, source, target):
        return pltpu.make_async_remote_copy(
            src_ref=planes.at[pl.ds(p * slab, slab)], dst_ref=t_buf.at[source],
            send_sem=t_send.at[d], recv_sem=t_recv.at[d],
            device_id=(target, p), device_id_type=MESH,
        )

    def t_sends(act):
        for d in range(1, tn):
            target = t + d if d % 2 else t - d

            @pl.when((target >= 0) & (target < tn))
            def send():
                act(t_copy(d, t, target))

    def t_arrivals():
        for d in range(1, tn):
            source = t - d if d % 2 else t + d

            @pl.when((source >= 0) & (source < tn))
            def arrived():
                t_copy(d, source, t).wait_recv()

    def a_copy(s, target, r):
        return pltpu.make_async_remote_copy(
            src_ref=a_buf.at[s, r], dst_ref=a_buf.at[s, r],
            send_sem=a_send.at[s, target, r], recv_sem=a_recv.at[s, r],
            device_id=(target, p), device_id_type=MESH,
        )

    def a_route(r, act, straight):
        for s in range(tn - 1):
            for target in range(s + 1, tn):
                if s % 2 == 0 or target == s + 1:

                    @pl.when(t == s)
                    def direct():
                        act(a_copy(s, target, r))

                elif straight:

                    @pl.when((t == s) & (core >= 0))
                    def far():
                        act(a_copy(s, target, r))

    def a_onward(r, act, wait, straight):
        for s in range(1, tn - 2, 2):

            @pl.when((t == s + 1) & ((core < 0) if straight else True))
            def onward():
                if wait:
                    a_copy(s, s + 1, r).wait_recv()
                for target in range(s + 2, tn):
                    act(a_copy(s, target, r))

    def a_arrivals(r):
        straight = r >= slab - HELD
        for s in range(tn - 1):
            here = t > s
            if s % 2 == 1 and s + 2 < tn:
                here = (t > s + 1) | ((t == s + 1) & (core >= 0)) if straight else t > s + 1

            @pl.when(here)
            def arrived():
                a_copy(s, s + 1, r).wait_recv()

    def start(copy):
        copy.start()

    def sent(copy):
        copy.wait_send()

    def g_up(source, target):
        return pltpu.make_async_remote_copy(
            src_ref=g_col.at[source], dst_ref=g_col.at[source],
            send_sem=g_send.at[target], recv_sem=g_recv.at[source],
            device_id=(target, p), device_id_type=MESH,
        )

    def g_share(d):
        return pltpu.make_async_remote_copy(
            src_ref=g_col, dst_ref=g_buf.at[p],
            send_sem=share_send, recv_sem=share_recv,
            device_id=(t, lax.rem(p + d, pn)), device_id_type=MESH,
        )

    def g_shares():
        every = g_buf.at[pl.ds(0, pn - 1)]
        return pltpu.make_async_remote_copy(
            src_ref=every, dst_ref=every, send_sem=share_send, recv_sem=share_recv,
            device_id=(t, partner), device_id_type=MESH,
        )

    group_of = lax.broadcasted_iota(jnp.int32, (rows, lanes), 1) // length
    per_block = groups // occupied_ref.shape[0]
    lane_group = lax.broadcasted_iota(jnp.int32, (length, lanes), 1) // length
    occ = 0.25 + 0.75 * occupied_ref[0].astype(jnp.float32) * jnp.ones((length, lanes), jnp.float32)
    for i in range(1, occupied_ref.shape[0]):
        level = 0.25 + 0.75 * occupied_ref[i].astype(jnp.float32)
        occ = jnp.where(lane_group >= i * per_block, level, occ)

    at_group = [group_of == g for g in range(groups)]
    def pick(options):
        chosen = options[0]
        for g in range(1, groups):
            chosen = jnp.where(at_group[g], options[g], chosen)
        return chosen

    def turn(value, steps):
        steps = steps % groups
        return value if steps == 0 else pltpu.roll(value, steps * length, 1)

    plane_rows = length * rows

    weights_load.wait()
    psi_load(0).wait()
    for a in range(rows):
        plane_load(0, a).wait()

    @pl.loop(0, length // FORWARD)
    def forward(i):
        @pl.when(i == early // FORWARD)
        def rest():
            psi_load(1).wait()
            for a in range(rows):
                plane_load(1, a).wait()

        density = []
        for j in range(FORWARD):
            x = i * FORWARD + j
            for q in range(length // groups):
                v = planes[x, :, q * lanes : (q + 1) * lanes]
                turned = [turn(v, s) for s in range(groups)]
                for g in range(groups):
                    y = q * groups + g
                    spread = pick([turned[(h - g) % groups] for h in range(groups)])
                    density.append(spread * psi_ref[x, y : y + 1, :])
        waves = split_product(jnp.concatenate(density, axis=0), weights_ref[...])
        for j in range(FORWARD):
            wave = waves[j * plane_rows : (j + 1) * plane_rows]
            modes = flat_dft([wave[y * rows : (y + 1) * rows] for y in range(length)])
            for m in range(length):
                spec[i * FORWARD + j, m] = modes[m]

    for x in range(length):
        psi_ref[x] = psi_ref[x] * occ
    table_load.wait()
    pl.semaphore_wait(barrier, tn + pn - 2)
    t_sends(start)

    @pl.loop(0, length // MIDDLE)
    def middle(step):
        half = length // 2
        for j in range(MIDDLE):
            m = step * MIDDLE + j
            modes = flat_dft([spec[x, m] for x in range(length)])
            scaled = []
            for i in range(length):
                k = i if i <= half else i - half
                scaled.append(modes[i] * table_ref[m, k : k + 1, :])
            values = flat_dft_transposed(scaled)
            for x in range(length):
                spec[x, m] = values[x]

    per = chips // BACKWARD

    @pl.loop(0, 2 * slab * per)
    def backward(n):
        i = n // per
        first = lax.rem(n, per) * BACKWARD
        odd = lax.rem(i, 2)
        last = i == 2 * slab - 1
        away = (i == 0) | ((odd == 1) & jnp.logical_not(last))
        r = jnp.where(away, (i + 1) // 2, jnp.where(last, slab - 1, i // 2 - 1))
        side = jnp.where(away, 1 - core, core)
        if chips == BACKWARD == 4:
            order = [chips - 1 - chip, lax.rem(chip + 2, chips), chip + 1 - 2 * lax.rem(chip, 2), chip]
        else:
            order = [lax.rem(chip + 1 + first + j, chips) for j in range(BACKWARD)]
        owners = [2 * c + side for c in order]
        values = []
        for q in owners:
            values += flat_dft_transposed([spec[q * slab + r, m] for m in range(length)])
        potentials = split_product(jnp.concatenate(values, axis=0), weights_ref[...])
        for j, owner in enumerate(owners):
            x = owner * slab + r
            potential = potentials[j * plane_rows : (j + 1) * plane_rows]
            for q in range(length // groups):
                terms = []
                for g in range(groups):
                    y = q * groups + g
                    terms.append(potential[y * rows : (y + 1) * rows] * psi_ref[x, y : y + 1, :])
                total = None
                for s in range(groups):
                    moved = turn(pick([terms[(h - s) % groups] for h in range(groups)]), -s)
                    total = moved if total is None else total + moved
                part[x, :, q * lanes : (q + 1) * lanes] = total

        @pl.when(away)
        def to_partner():
            for owner in owners:
                pair_copy(owner, r).start()

        @pl.when(jnp.logical_not(away))
        def to_owners():
            for j, owner in enumerate(owners):
                pair_copy(owner, r).wait_recv()

                @pl.when(first + j < chips - 1)
                def send():
                    x = owner * slab + r
                    part[x] = part[x] + pair_buf[owner // 2, r]
                    rs_copy(owner // 2, chip, r).start()

    t_buf[t] = planes[pl.ds(p * slab, slab)]
    for s in range(1, tn):

        @pl.when(s > t)
        def clear():
            a_buf[s] = jnp.zeros(a_buf.shape[1:], jnp.float32)
            g_col[s] = jnp.zeros(g_col.shape[1:], jnp.float32)

    gram_ref[...] = jnp.zeros_like(gram_ref)
    def add_gram(r):
        every = jnp.concatenate([t_buf[s, r] for s in range(tn)], axis=0)
        gram_ref[...] += lax.dot_general(
            a_buf[t, r], every, (((1,), (1,)), ((), ())),
            precision=HIGHEST, preferred_element_type=jnp.float32,
        )

    @pl.loop(0, slab)
    def reduce(r):
        own = part[p * slab + r] + pair_buf[chip, r]
        for d in range(1, chips):
            c = lax.rem(chip + d, chips)
            rs_copy(c, c, r).wait_recv()
            own = own + rs_buf[c, r]
        a_buf[t, r] = own

        @pl.when(r < slab - HELD)
        def at_once():
            a_route(r, start, False)

        @pl.when(r == 1)
        def met():
            t_arrivals()

        @pl.when(r > 0)
        def earlier():
            add_gram(r - 1)

    add_gram(slab - 1)
    gram = gram_ref[...] * (1.0 / all_cells)
    fold = 128 // total_rows
    short = rows // fold
    g_col[t] = jnp.concatenate([gram[i * short : (i + 1) * short] for i in range(fold)], axis=1)
    for target in reversed(range(1, tn)):

        @pl.when(t < target)
        def upward():
            g_up(t, target).start()

    for r in range(slab - HELD):
        a_onward(r, start, True, False)
    for r in range(slab - HELD, slab):
        a_route(r, start, True)
    t_sends(sent)

    @pl.loop(0, slab)
    def drain(r):
        for c in range(chips):
            pair_copy(2 * c + 1 - core, r).wait_send()
        for d in range(1, chips):
            rs_copy(lax.rem(chip + d, chips), chip, r).wait_send()

    for r in range(slab - HELD, slab):
        a_onward(r, start, True, True)

    for s in range(tn - 1):

        @pl.when(t > s)
        def below():
            g_up(s, t).wait_recv()

    for d in range(1, pn):
        g_share(d).start()
    g_buf[p] = g_col[...]
    for target in range(1, tn):

        @pl.when(t < target)
        def ended():
            g_up(t, target).wait_send()

    for r in range(slab - HELD):
        a_route(r, sent, False)
        a_onward(r, sent, False, False)
    g_shares().wait_recv()
    blocks = []
    summed = g_buf[0]
    for q in range(1, pn):
        summed = summed + g_buf[q]
    for s in range(tn):
        blocks += [summed[s, :, i * total_rows : (i + 1) * total_rows] for i in range(fold)]
    square = jnp.concatenate(blocks, axis=0)
    square = jnp.concatenate(
        [square, jnp.zeros((total_rows, width - total_rows), jnp.float32)], axis=1
    )
    row_of = lax.broadcasted_iota(jnp.int32, (total_rows, width), 0)
    lane_of = lax.broadcasted_iota(jnp.int32, (total_rows, width), 1)
    row_block, lane_block = row_of // rows, lane_of // rows
    apart = lane_block - row_block
    odd = lax.rem(jnp.abs(apart), 2) == 1
    held = (apart == 0) | ((apart < 0) & odd) | ((apart > 0) & jnp.logical_not(odd))
    held = held & (row_block <= t) & (lane_block <= t)
    square = jnp.where(held, square, 0.0)
    padded = jnp.concatenate([square, jnp.zeros((width - total_rows, width), jnp.float32)], axis=0)
    both = square + jnp.transpose(padded)[:total_rows]
    symmetric = jnp.where(apart == 0, 0.5 * both, both)
    unit = (lane_of == row_of + total_rows) | ((lane_of == row_of) & (row_block > t))
    work = jnp.where(unit, 1.0, symmetric)
    line_of = lax.broadcasted_iota(jnp.int32, (PIVOTS, width), 0)
    strips = [work[k : k + PIVOTS, :] for k in range(0, total_rows, PIVOTS)]
    for k, strip in enumerate(strips):
        lines = [jnp.broadcast_to(strip[i : i + 1, :], strip.shape) for i in range(PIVOTS)]
        lane = [k * PIVOTS + i for i in range(PIVOTS)]
        corner = [
            [jnp.broadcast_to(line[:, h : h + 1], line.shape) for h in lane] for line in lines
        ]
        below = range(k + 1, len(strips))
        columns = [
            [jnp.broadcast_to(strips[g][:, h : h + 1], strip.shape) for g in below] for h in lane
        ]
        done = strip
        for i in range(PIVOTS):
            pivot = corner[i][i]
            inverse = 1.0 / pivot
            scaled = lines[i] * inverse
            done = jnp.where(line_of == i, lines[i] * (1.0 / jnp.sqrt(pivot)), done)
            for m in range(i + 1, PIVOTS):
                factor = corner[i][m] * inverse
                lines[m] = lines[m] - corner[i][m] * scaled
                for h in range(m, PIVOTS):
                    corner[m][h] = corner[m][h] - factor * corner[i][h]
                columns[m] = [c - d * factor for c, d in zip(columns[m], columns[i])]
            for g, column in zip(below, columns[i]):
                strips[g] = strips[g] - column * scaled
        strips[k] = done
    work = jnp.concatenate(strips, axis=0)
    keeping = (row_of < retained_ref[0]).astype(jnp.float32)
    inv_ref[...] = work * keeping
    mine = inv_ref[pl.ds(pl.multiple_of(t * rows, rows), rows), :][:, total_rows : 2 * total_rows]
    for x in range(slab):
        a_arrivals(x)
        every = jnp.concatenate([a_buf[s, x] for s in range(tn)], axis=0)
        out_ref[:, x, :] = jnp.dot(
            mine, every, precision=HIGHEST, preferred_element_type=jnp.float32
        )

    g_shares().wait_send()
    for r in range(slab - HELD, slab):
        a_route(r, sent, True)
        a_onward(r, sent, False, True)


def constants(length, groups):
    i = np.arange(length)
    phase = 2.0 * np.pi / length * (i[:, None] * i[None, :] % length)
    cas = np.kron(np.eye(groups), np.cos(phase) + np.sin(phase)).astype(np.float32)
    high = cas.astype(jnp.bfloat16)
    low = (cas - high.astype(np.float32)).astype(jnp.bfloat16)
    weights = np.concatenate([np.concatenate([high, low], 1)] * 2, 0)
    signed = np.where(i < length // 2, i, i - length)
    half = length // 2
    k = np.arange(half + 1)
    wave = (2.0 * np.pi / length) ** 2
    total = wave * ((k**2)[:, None, None] + (k**2)[None, :, None] + (signed**2)[None, None, :])
    coulomb = np.where(total > 0, 4 * np.pi / np.where(total > 0, total, 1.0), 0.0)
    fold = np.where((k == 0) | (k == half), 1.0, 2.0)
    coulomb = coulomb * fold[:, None, None] * fold[None, :, None] / length**3
    order = np.concatenate([np.arange(half + 1), np.arange(1, half)])
    table = np.tile(coulomb[order], (1, 1, groups)).astype(np.float32)
    return weights, table


def shards(tn, pn, targets, partners, occupied, retained):
    rows, length, cells = targets.shape
    lanes = partners.shape[2]
    groups = lanes // length
    slab = length // pn
    weights, table = constants(length, groups)
    total_rows = tn * rows
    width = -(-2 * total_rows // 128) * 128
    vmem = pl.BlockSpec(memory_space=pltpu.VMEM)
    smem = pl.BlockSpec(memory_space=pltpu.SMEM)
    hbm = pl.BlockSpec(memory_space=pl.ANY)
    planes = pltpu.VMEM((length, rows, cells), jnp.float32)
    block = pltpu.VMEM((tn, slab, rows, cells), jnp.float32)
    received = pltpu.VMEM((pn // 2, slab, rows, cells), jnp.float32)
    return pl.pallas_call(
        functools.partial(kernel, tn, pn),
        out_shape=pltpu.VMEM((rows, slab, cells), jnp.float32),
        in_specs=[hbm, hbm, hbm, hbm, smem, smem],
        out_specs=vmem,
        scratch_shapes=[
            planes,
            pltpu.VMEM(partners.shape, jnp.float32),
            pltpu.VMEM(weights.shape, weights.dtype),
            pltpu.VMEM(table.shape, jnp.float32),
            pltpu.VMEM((length, length + 1, rows, lanes), jnp.float32),
            planes,
            received,
            received,
            block,
            block,
            pltpu.VMEM((rows, total_rows), jnp.float32),
            pltpu.VMEM((tn, rows * total_rows // 128, 128), jnp.float32),
            pltpu.VMEM((pn, tn, rows * total_rows // 128, 128), jnp.float32),
            pltpu.VMEM((total_rows, width), jnp.float32),
        ],
        compiler_params=pltpu.CompilerParams(collective_id=0, has_side_effects=True),
        name="exchange",
    )(targets, partners, jnp.asarray(weights), jnp.asarray(table), occupied, retained)


def solution(mesh):
    return jax.shard_map(
        functools.partial(shards, mesh.shape["tgt"], mesh.shape["ptr"]),
        mesh=mesh,
        in_specs=(P("tgt", None, None), P(None, None, "ptr"), P("ptr"), P()),
        out_specs=P("tgt", "ptr", None),
        check_vma=False,
    )
```

```python
import functools
import math

import jax
import jax.numpy as jnp
import numpy as np
from jax import lax
from jax.experimental import pallas as pl
from jax.experimental.pallas import tpu as pltpu
from jax.sharding import PartitionSpec as P

HIGHEST = lax.Precision.HIGHEST
MESH = pl.DeviceIdType.MESH
FORWARD = 8
BACKWARD = 4
PIVOTS = 8
MIDDLE = 2
HELD = 2
NEAR = 2


def turned_by(n, k, re, im):
    c, s = math.cos(2 * math.pi * k / n), math.sin(2 * math.pi * k / n)
    return c * re + s * im, c * im - s * re


def real_dft(values):
    n = len(values)
    if n == 1:
        return [values[0]], [None]
    if n == 2:
        return [values[0] + values[1], values[0] - values[1]], [None, None]
    half, quarter, eighth = n // 2, n // 4, n // 8
    even_re, even_im = real_dft(values[0::2])
    one_re, one_im = real_dft(values[1::4])
    three_re, three_im = real_dft(values[3::4])
    re, im = [None] * (half + 1), [None] * (half + 1)
    total = one_re[0] + three_re[0]
    re[0], re[half] = even_re[0] + total, even_re[0] - total
    re[quarter], im[quarter] = even_re[quarter], three_re[0] - one_re[0]
    for k in range(1, eighth + 1):
        if 2 * k == quarter:
            c = math.sqrt(0.5)
            a, b = c * (one_re[k] - three_re[k]), c * (one_re[k] + three_re[k])
            re[k], re[half - k] = even_re[k] + a, even_re[k] - a
            im[k], im[half - k] = even_im[k] - b, -b - even_im[k]
            continue
        one = turned_by(n, k, one_re[k], one_im[k])
        three = turned_by(n, 3 * k, three_re[k], three_im[k])
        sum_re, sum_im = one[0] + three[0], one[1] + three[1]
        gap_re, gap_im = one[0] - three[0], one[1] - three[1]
        re[k], re[half - k] = even_re[k] + sum_re, even_re[k] - sum_re
        im[k], im[half - k] = even_im[k] + sum_im, sum_im - even_im[k]
        mirror = quarter - k
        re[quarter + k], re[mirror] = even_re[mirror] + gap_im, even_re[mirror] - gap_im
        im[quarter + k], im[mirror] = -gap_re - even_im[mirror], even_im[mirror] - gap_re
    return re, im


def real_dft_transposed(re, im):
    half = len(re) - 1
    if half == 0:
        return [re[0]]
    if half == 1:
        return [re[0] + re[1], re[0] - re[1]]
    n = 2 * half
    quarter, eighth = half // 2, half // 4
    even_re, even_im = [None] * (quarter + 1), [None] * (quarter + 1)
    one_re, one_im = [None] * (eighth + 1), [None] * (eighth + 1)
    three_re, three_im = [None] * (eighth + 1), [None] * (eighth + 1)
    even_re[0], total = re[0] + re[half], re[0] - re[half]
    even_re[quarter] = re[quarter]
    one_re[0], three_re[0] = total - im[quarter], total + im[quarter]
    for k in range(1, eighth + 1):
        sum_re, even_re[k] = re[k] - re[half - k], re[k] + re[half - k]
        sum_im, even_im[k] = im[k] + im[half - k], im[k] - im[half - k]
        if 2 * k == quarter:
            c = math.sqrt(0.5)
            one_re[k], three_re[k] = c * (sum_re - sum_im), -c * (sum_re + sum_im)
            continue
        mirror = quarter - k
        even_re[mirror], gap_im = re[quarter + k] + re[mirror], re[quarter + k] - re[mirror]
        even_im[mirror] = im[mirror] - im[quarter + k]
        gap_re = -(im[quarter + k] + im[mirror])
        one = sum_re + gap_re, sum_im + gap_im
        three = sum_re - gap_re, sum_im - gap_im
        one_re[k], one_im[k] = turned_by(n, -k, *one)
        three_re[k], three_im[k] = turned_by(n, -3 * k, *three)
    values = [None] * n
    values[0::2] = real_dft_transposed(even_re, even_im)
    values[1::4] = real_dft_transposed(one_re, one_im)
    values[3::4] = real_dft_transposed(three_re, three_im)
    return values


def flat_dft(values):
    re, im = real_dft(values)
    return re + im[1:-1]


def flat_dft_transposed(modes):
    half = len(modes) // 2
    return real_dft_transposed(modes[: half + 1], [None] + modes[half + 1 :] + [None])


def split_product(field, weights):
    width = field.shape[1]
    high = field.astype(jnp.bfloat16)
    low = (field - high.astype(jnp.float32)).astype(jnp.bfloat16)
    both = jnp.dot(
        jnp.concatenate([high, low], axis=1), weights, preferred_element_type=jnp.float32
    )
    return both[:, :width] + both[:, width:]


def kernel(
    tn, pn, t_hbm, psi_hbm, weights_hbm, table_hbm, occupied_ref, retained_ref, out_ref,
    planes, psi_ref, weights_ref, table_ref, spec, part, pair_buf, rs_buf, t_buf, a_buf,
    gram_ref, g_col, g_near, g_buf, inv_ref,
):
    slab = planes.shape[0] // pn
    rows = planes.shape[1]
    dma = pltpu.SemaphoreType.DMA
    pl.run_scoped(
        functools.partial(
            exchange, tn, pn, t_hbm, psi_hbm, weights_hbm, table_hbm, occupied_ref, retained_ref,
            out_ref, planes, psi_ref, weights_ref, table_ref, spec, part, pair_buf, rs_buf, t_buf,
            a_buf, gram_ref, g_col, g_near, g_buf, inv_ref,
        ),
        dma((2, rows)), dma((4,)), dma((pn // 2, slab)), dma((pn // 2, slab)),
        dma((pn // 2, slab)), dma((pn // 2, slab)), dma((tn,)), dma((tn,)),
        dma((tn, tn, slab)), dma((tn, slab)), dma((tn,)), dma((tn,)), dma, dma, dma((NEAR,)), dma((NEAR,)),
    )


def exchange(
    tn, pn, t_hbm, psi_hbm, weights_hbm, table_hbm, occupied_ref, retained_ref, out_ref,
    planes, psi_ref, weights_ref, table_ref, spec, part, pair_buf, rs_buf, t_buf, a_buf,
    gram_ref, g_col, g_near, g_buf, inv_ref,
    plane_sem, load_sem, pair_send, pair_recv, rs_send, rs_recv, t_send, t_recv,
    a_send, a_recv, g_send, g_recv, share_send, share_recv,
    near_send, near_recv,
):
    t, p = lax.axis_index("tgt"), lax.axis_index("ptr")
    length, rows, cells = planes.shape
    lanes = psi_ref.shape[2]
    groups = lanes // length
    slab = length // pn
    all_cells = length * cells
    total_rows = tn * rows
    width = inv_ref.shape[1]
    chips = pn // 2
    chip, core = p // 2, lax.rem(p, 2)
    partner = p + 1 - 2 * core
    early = length // 4

    def plane_load(c, a):
        xs = pl.ds(0, early) if c == 0 else pl.ds(early, length - early)
        return pltpu.make_async_copy(t_hbm.at[a, xs, :], planes.at[xs, a, :], plane_sem.at[c, a])

    def psi_load(c):
        xs = pl.ds(0, early) if c == 0 else pl.ds(early, length - early)
        return pltpu.make_async_copy(psi_hbm.at[xs], psi_ref.at[xs], load_sem.at[c])

    weights_load = pltpu.make_async_copy(weights_hbm, weights_ref, load_sem.at[2])
    table_load = pltpu.make_async_copy(table_hbm, table_ref, load_sem.at[3])

    weights_load.start()
    for c in range(2):
        psi_load(c).start()
        for a in range(rows):
            plane_load(c, a).start()
    table_load.start()

    barrier = pltpu.get_barrier_semaphore()
    for tt in range(tn):

        @pl.when(t != tt)
        def column():
            pl.semaphore_signal(barrier, inc=1, device_id=(tt, p), device_id_type=MESH)

    for d in range(1, pn):
        pl.semaphore_signal(
            barrier, inc=1, device_id=(t, lax.rem(p + d, pn)), device_id_type=MESH
        )

    for k in range(1, NEAR + 1):

        @pl.when(t >= k)
        def senders():
            for d in range(1, pn):
                pl.semaphore_signal(
                    barrier, inc=1, device_id=(t - k, lax.rem(p + d, pn)), device_id_type=MESH
                )

    def pair_copy(q, r):
        return pltpu.make_async_remote_copy(
            src_ref=part.at[q * slab + r], dst_ref=pair_buf.at[q // 2, r],
            send_sem=pair_send.at[q // 2, r], recv_sem=pair_recv.at[q // 2, r],
            device_id=(t, partner), device_id_type=MESH,
        )

    def rs_copy(c, slot, r):
        q = 2 * c + core
        return pltpu.make_async_remote_copy(
            src_ref=part.at[q * slab + r], dst_ref=rs_buf.at[slot, r],
            send_sem=rs_send.at[c, r], recv_sem=rs_recv.at[slot, r],
            device_id=(t, q), device_id_type=MESH,
        )

    def t_copy(d, source, target):
        return pltpu.make_async_remote_copy(
            src_ref=planes.at[pl.ds(p * slab, slab)], dst_ref=t_buf.at[source],
            send_sem=t_send.at[d], recv_sem=t_recv.at[d],
            device_id=(target, p), device_id_type=MESH,
        )

    def t_sends(act):
        for d in range(1, tn):
            target = t + d if d % 2 else t - d

            @pl.when((target >= 0) & (target < tn))
            def send():
                act(t_copy(d, t, target))

    def t_arrivals():
        for d in range(1, tn):
            source = t - d if d % 2 else t + d

            @pl.when((source >= 0) & (source < tn))
            def arrived():
                t_copy(d, source, t).wait_recv()

    def a_copy(s, target, r):
        return pltpu.make_async_remote_copy(
            src_ref=a_buf.at[s, r], dst_ref=a_buf.at[s, r],
            send_sem=a_send.at[s, target, r], recv_sem=a_recv.at[s, r],
            device_id=(target, p), device_id_type=MESH,
        )

    def a_route(r, act, straight):
        for s in range(tn - 1):
            for target in range(s + 1, tn):
                if s % 2 == 0 or target == s + 1:

                    @pl.when(t == s)
                    def direct():
                        act(a_copy(s, target, r))

                elif straight:

                    @pl.when((t == s) & (core >= 0))
                    def far():
                        act(a_copy(s, target, r))

    def a_onward(r, act, wait, straight):
        for s in range(1, tn - 2, 2):

            @pl.when((t == s + 1) & ((core < 0) if straight else True))
            def onward():
                if wait:
                    a_copy(s, s + 1, r).wait_recv()
                for target in range(s + 2, tn):
                    act(a_copy(s, target, r))

    def a_arrivals(r):
        straight = r >= slab - HELD
        for s in range(tn - 1):
            here = t > s
            if s % 2 == 1 and s + 2 < tn:
                here = (t > s + 1) | ((t == s + 1) & (core >= 0)) if straight else t > s + 1

            @pl.when(here)
            def arrived():
                a_copy(s, s + 1, r).wait_recv()

    def start(copy):
        copy.start()

    def sent(copy):
        copy.wait_send()

    def g_up(source, target):
        return pltpu.make_async_remote_copy(
            src_ref=g_col.at[source], dst_ref=g_col.at[source],
            send_sem=g_send.at[target], recv_sem=g_recv.at[source],
            device_id=(target, p), device_id_type=MESH,
        )

    def g_next(k, d):
        return pltpu.make_async_remote_copy(
            src_ref=g_col.at[t], dst_ref=g_near.at[k - 1, p],
            send_sem=near_send.at[k - 1], recv_sem=near_recv.at[k - 1],
            device_id=(t + k, lax.rem(p + d, pn)), device_id_type=MESH,
        )

    def g_nears(k):
        return pltpu.make_async_remote_copy(
            src_ref=g_near.at[k - 1], dst_ref=g_near.at[k - 1],
            send_sem=near_send.at[k - 1], recv_sem=near_recv.at[k - 1],
            device_id=(t, partner), device_id_type=MESH,
        )

    def g_share(d):
        return pltpu.make_async_remote_copy(
            src_ref=g_col, dst_ref=g_buf.at[p],
            send_sem=share_send, recv_sem=share_recv,
            device_id=(t, lax.rem(p + d, pn)), device_id_type=MESH,
        )

    def g_shares():
        every = g_buf.at[pl.ds(0, pn - 1)]
        return pltpu.make_async_remote_copy(
            src_ref=every, dst_ref=every, send_sem=share_send, recv_sem=share_recv,
            device_id=(t, partner), device_id_type=MESH,
        )

    group_of = lax.broadcasted_iota(jnp.int32, (rows, lanes), 1) // length
    per_block = groups // occupied_ref.shape[0]
    lane_group = lax.broadcasted_iota(jnp.int32, (length, lanes), 1) // length
    occ = 0.25 + 0.75 * occupied_ref[0].astype(jnp.float32) * jnp.ones((length, lanes), jnp.float32)
    for i in range(1, occupied_ref.shape[0]):
        level = 0.25 + 0.75 * occupied_ref[i].astype(jnp.float32)
        occ = jnp.where(lane_group >= i * per_block, level, occ)

    at_group = [group_of == g for g in range(groups)]
    def pick(options):
        chosen = options[0]
        for g in range(1, groups):
            chosen = jnp.where(at_group[g], options[g], chosen)
        return chosen

    def turn(value, steps):
        steps = steps % groups
        return value if steps == 0 else pltpu.roll(value, steps * length, 1)

    plane_rows = length * rows

    weights_load.wait()
    psi_load(0).wait()
    for a in range(rows):
        plane_load(0, a).wait()

    @pl.loop(0, length // FORWARD)
    def forward(i):
        @pl.when(i == early // FORWARD)
        def rest():
            psi_load(1).wait()
            for a in range(rows):
                plane_load(1, a).wait()

        density = []
        for j in range(FORWARD):
            x = i * FORWARD + j
            for q in range(length // groups):
                v = planes[x, :, q * lanes : (q + 1) * lanes]
                turned = [turn(v, s) for s in range(groups)]
                for g in range(groups):
                    y = q * groups + g
                    spread = pick([turned[(h - g) % groups] for h in range(groups)])
                    density.append(spread * psi_ref[x, y : y + 1, :])
        waves = split_product(jnp.concatenate(density, axis=0), weights_ref[...])
        for j in range(FORWARD):
            wave = waves[j * plane_rows : (j + 1) * plane_rows]
            modes = flat_dft([wave[y * rows : (y + 1) * rows] for y in range(length)])
            for m in range(length):
                spec[i * FORWARD + j, m] = modes[m]

    for x in range(length):
        psi_ref[x] = psi_ref[x] * occ
    table_load.wait()
    pl.semaphore_wait(barrier, tn + pn - 2 + (pn - 1) * jnp.minimum(NEAR, tn - 1 - t))
    t_sends(start)

    @pl.loop(0, length // MIDDLE)
    def middle(step):
        half = length // 2
        for j in range(MIDDLE):
            m = step * MIDDLE + j
            modes = flat_dft([spec[x, m] for x in range(length)])
            scaled = []
            for i in range(length):
                k = i if i <= half else i - half
                scaled.append(modes[i] * table_ref[m, k : k + 1, :])
            values = flat_dft_transposed(scaled)
            for x in range(length):
                spec[x, m] = values[x]

    per = chips // BACKWARD

    @pl.loop(0, 2 * slab * per)
    def backward(n):
        i = n // per
        first = lax.rem(n, per) * BACKWARD
        odd = lax.rem(i, 2)
        last = i == 2 * slab - 1
        away = (i == 0) | ((odd == 1) & jnp.logical_not(last))
        r = jnp.where(away, (i + 1) // 2, jnp.where(last, slab - 1, i // 2 - 1))
        side = jnp.where(away, 1 - core, core)
        if chips == BACKWARD == 4:
            order = [chips - 1 - chip, lax.rem(chip + 2, chips), chip + 1 - 2 * lax.rem(chip, 2), chip]
        else:
            order = [lax.rem(chip + 1 + first + j, chips) for j in range(BACKWARD)]
        owners = [2 * c + side for c in order]
        values = []
        for q in owners:
            values += flat_dft_transposed([spec[q * slab + r, m] for m in range(length)])
        potentials = split_product(jnp.concatenate(values, axis=0), weights_ref[...])
        for j, owner in enumerate(owners):
            x = owner * slab + r
            potential = potentials[j * plane_rows : (j + 1) * plane_rows]
            for q in range(length // groups):
                terms = []
                for g in range(groups):
                    y = q * groups + g
                    terms.append(potential[y * rows : (y + 1) * rows] * psi_ref[x, y : y + 1, :])
                total = None
                for s in range(groups):
                    moved = turn(pick([terms[(h - s) % groups] for h in range(groups)]), -s)
                    total = moved if total is None else total + moved
                part[x, :, q * lanes : (q + 1) * lanes] = total

        @pl.when(away)
        def to_partner():
            for owner in owners:
                pair_copy(owner, r).start()

        @pl.when(jnp.logical_not(away))
        def to_owners():
            for j, owner in enumerate(owners):
                pair_copy(owner, r).wait_recv()

                @pl.when(first + j < chips - 1)
                def send():
                    x = owner * slab + r
                    part[x] = part[x] + pair_buf[owner // 2, r]
                    rs_copy(owner // 2, chip, r).start()

    t_buf[t] = planes[pl.ds(p * slab, slab)]
    for s in range(1, tn):

        @pl.when(s > t)
        def clear():
            a_buf[s] = jnp.zeros(a_buf.shape[1:], jnp.float32)

    for s in range(tn):

        @pl.when((s > t) | ((s < t) & (s >= t - NEAR)))
        def unused():
            g_col[s] = jnp.zeros(g_col.shape[1:], jnp.float32)

    gram_ref[...] = jnp.zeros_like(gram_ref)
    def add_gram(r):
        every = jnp.concatenate([t_buf[s, r] for s in range(tn)], axis=0)
        gram_ref[...] += lax.dot_general(
            a_buf[t, r], every, (((1,), (1,)), ((), ())),
            precision=HIGHEST, preferred_element_type=jnp.float32,
        )

    @pl.loop(0, slab)
    def reduce(r):
        own = part[p * slab + r] + pair_buf[chip, r]
        for d in range(1, chips):
            c = lax.rem(chip + d, chips)
            rs_copy(c, c, r).wait_recv()
            own = own + rs_buf[c, r]
        a_buf[t, r] = own

        @pl.when(r < slab - HELD)
        def at_once():
            a_route(r, start, False)

        @pl.when(r == 1)
        def met():
            t_arrivals()

        @pl.when(r > 0)
        def earlier():
            add_gram(r - 1)

    add_gram(slab - 1)
    gram = gram_ref[...] * (1.0 / all_cells)
    fold = 128 // total_rows
    short = rows // fold
    g_col[t] = jnp.concatenate([gram[i * short : (i + 1) * short] for i in range(fold)], axis=1)
    for k in reversed(range(1, NEAR + 1)):

        @pl.when(t + k < tn)
        def upper():
            for d in reversed(range(pn)):
                g_next(k, d).start()

    for target in reversed(range(1, tn)):

        @pl.when(t + NEAR < target)
        def upward():
            g_up(t, target).start()

    for r in range(slab - HELD):
        a_onward(r, start, True, False)
    for r in range(slab - HELD, slab):
        a_route(r, start, True)
    t_sends(sent)

    @pl.loop(0, slab)
    def drain(r):
        for c in range(chips):
            pair_copy(2 * c + 1 - core, r).wait_send()
        for d in range(1, chips):
            rs_copy(lax.rem(chip + d, chips), chip, r).wait_send()

    for r in range(slab - HELD, slab):
        a_onward(r, start, True, True)

    for s in range(tn - 1):

        @pl.when(t > s + NEAR)
        def below():
            g_up(s, t).wait_recv()

    for d in range(1, pn):
        g_share(d).start()
    g_buf[p] = g_col[...]
    for target in range(1, tn):

        @pl.when(t + NEAR < target)
        def ended():
            g_up(t, target).wait_send()

    for k in range(1, NEAR + 1):

        @pl.when(t + k < tn)
        def passed():
            g_nears(k).wait_send()

    for r in range(slab - HELD):
        a_route(r, sent, False)
        a_onward(r, sent, False, False)
    g_shares().wait_recv()

    for k in range(1, NEAR + 1):

        @pl.when(t >= k)
        def lower():
            g_nears(k).wait_recv()

    blocks = []
    summed = g_buf[0]
    for q in range(1, pn):
        summed = summed + g_buf[q]
    near = []
    for k in range(NEAR):
        total = g_near[k, 0]
        for q in range(1, pn):
            total = total + g_near[k, q]
        near.append(total)
    for s in range(tn):
        piece = summed[s]
        for k in range(NEAR):
            piece = piece + jnp.where(t == s + k + 1, near[k], 0.0)
        blocks += [piece[:, i * total_rows : (i + 1) * total_rows] for i in range(fold)]
    square = jnp.concatenate(blocks, axis=0)
    square = jnp.concatenate(
        [square, jnp.zeros((total_rows, width - total_rows), jnp.float32)], axis=1
    )
    row_of = lax.broadcasted_iota(jnp.int32, (total_rows, width), 0)
    lane_of = lax.broadcasted_iota(jnp.int32, (total_rows, width), 1)
    row_block, lane_block = row_of // rows, lane_of // rows
    apart = lane_block - row_block
    odd = lax.rem(jnp.abs(apart), 2) == 1
    held = (apart == 0) | ((apart < 0) & odd) | ((apart > 0) & jnp.logical_not(odd))
    held = held & (row_block <= t) & (lane_block <= t)
    square = jnp.where(held, square, 0.0)
    padded = jnp.concatenate([square, jnp.zeros((width - total_rows, width), jnp.float32)], axis=0)
    both = square + jnp.transpose(padded)[:total_rows]
    symmetric = jnp.where(apart == 0, 0.5 * both, both)
    unit = (lane_of == row_of + total_rows) | ((lane_of == row_of) & (row_block > t))
    work = jnp.where(unit, 1.0, symmetric)
    line_of = lax.broadcasted_iota(jnp.int32, (PIVOTS, width), 0)
    strips = [work[k : k + PIVOTS, :] for k in range(0, total_rows, PIVOTS)]
    for k, strip in enumerate(strips):
        lines = [jnp.broadcast_to(strip[i : i + 1, :], strip.shape) for i in range(PIVOTS)]
        lane = [k * PIVOTS + i for i in range(PIVOTS)]
        corner = [
            [jnp.broadcast_to(line[:, h : h + 1], line.shape) for h in lane] for line in lines
        ]
        below = range(k + 1, len(strips))
        columns = [
            [jnp.broadcast_to(strips[g][:, h : h + 1], strip.shape) for g in below] for h in lane
        ]
        done = strip
        for i in range(PIVOTS):
            pivot = corner[i][i]
            inverse = 1.0 / pivot
            scaled = lines[i] * inverse
            done = jnp.where(line_of == i, lines[i] * (1.0 / jnp.sqrt(pivot)), done)
            for m in range(i + 1, PIVOTS):
                factor = corner[i][m] * inverse
                lines[m] = lines[m] - corner[i][m] * scaled
                for h in range(m, PIVOTS):
                    corner[m][h] = corner[m][h] - factor * corner[i][h]
                columns[m] = [c - d * factor for c, d in zip(columns[m], columns[i])]
            for g, column in zip(below, columns[i]):
                strips[g] = strips[g] - column * scaled
        strips[k] = done
    work = jnp.concatenate(strips, axis=0)
    keeping = (row_of < retained_ref[0]).astype(jnp.float32)
    inv_ref[...] = work * keeping
    mine = inv_ref[pl.ds(pl.multiple_of(t * rows, rows), rows), :][:, total_rows : 2 * total_rows]
    for x in range(slab):
        a_arrivals(x)
        every = jnp.concatenate([a_buf[s, x] for s in range(tn)], axis=0)
        out_ref[:, x, :] = jnp.dot(
            mine, every, precision=HIGHEST, preferred_element_type=jnp.float32
        )

    g_shares().wait_send()
    for r in range(slab - HELD, slab):
        a_route(r, sent, True)
        a_onward(r, sent, False, True)


def constants(length, groups):
    i = np.arange(length)
    phase = 2.0 * np.pi / length * (i[:, None] * i[None, :] % length)
    cas = np.kron(np.eye(groups), np.cos(phase) + np.sin(phase)).astype(np.float32)
    high = cas.astype(jnp.bfloat16)
    low = (cas - high.astype(np.float32)).astype(jnp.bfloat16)
    weights = np.concatenate([np.concatenate([high, low], 1)] * 2, 0)
    signed = np.where(i < length // 2, i, i - length)
    half = length // 2
    k = np.arange(half + 1)
    wave = (2.0 * np.pi / length) ** 2
    total = wave * ((k**2)[:, None, None] + (k**2)[None, :, None] + (signed**2)[None, None, :])
    coulomb = np.where(total > 0, 4 * np.pi / np.where(total > 0, total, 1.0), 0.0)
    fold = np.where((k == 0) | (k == half), 1.0, 2.0)
    coulomb = coulomb * fold[:, None, None] * fold[None, :, None] / length**3
    order = np.concatenate([np.arange(half + 1), np.arange(1, half)])
    table = np.tile(coulomb[order], (1, 1, groups)).astype(np.float32)
    return weights, table


def shards(tn, pn, targets, partners, occupied, retained):
    rows, length, cells = targets.shape
    lanes = partners.shape[2]
    groups = lanes // length
    slab = length // pn
    weights, table = constants(length, groups)
    total_rows = tn * rows
    width = -(-2 * total_rows // 128) * 128
    vmem = pl.BlockSpec(memory_space=pltpu.VMEM)
    smem = pl.BlockSpec(memory_space=pltpu.SMEM)
    hbm = pl.BlockSpec(memory_space=pl.ANY)
    planes = pltpu.VMEM((length, rows, cells), jnp.float32)
    block = pltpu.VMEM((tn, slab, rows, cells), jnp.float32)
    received = pltpu.VMEM((pn // 2, slab, rows, cells), jnp.float32)
    return pl.pallas_call(
        functools.partial(kernel, tn, pn),
        out_shape=pltpu.VMEM((rows, slab, cells), jnp.float32),
        in_specs=[hbm, hbm, hbm, hbm, smem, smem],
        out_specs=vmem,
        scratch_shapes=[
            planes,
            pltpu.VMEM(partners.shape, jnp.float32),
            pltpu.VMEM(weights.shape, weights.dtype),
            pltpu.VMEM(table.shape, jnp.float32),
            pltpu.VMEM((length, length + 1, rows, lanes), jnp.float32),
            planes,
            received,
            received,
            block,
            block,
            pltpu.VMEM((rows, total_rows), jnp.float32),
            pltpu.VMEM((tn, rows * total_rows // 128, 128), jnp.float32),
            pltpu.VMEM((NEAR, pn, rows * total_rows // 128, 128), jnp.float32),
            pltpu.VMEM((pn, tn, rows * total_rows // 128, 128), jnp.float32),
            pltpu.VMEM((total_rows, width), jnp.float32),
        ],
        compiler_params=pltpu.CompilerParams(collective_id=0, has_side_effects=True),
        name="exchange",
    )(targets, partners, jnp.asarray(weights), jnp.asarray(table), occupied, retained)


def solution(mesh):
    return jax.shard_map(
        functools.partial(shards, mesh.shape["tgt"], mesh.shape["ptr"]),
        mesh=mesh,
        in_specs=(P("tgt", None, None), P(None, None, "ptr"), P("ptr"), P()),
        out_specs=P("tgt", "ptr", None),
        check_vma=False,
    )
```
